32 devices in a mesh: dp: 8 (over z, y), tensor: 4 (over x, core).
Axes of the slice: x: 2, y: 2, z: 4, core: 2. Of those that a mesh axis runs over, the one named last changes fastest.
Arguments:
- hidden_in: bfloat16 [16384, 768], P(('dp', 'tensor')), may hold values from -6 to 6
- earlier: bfloat16 [4, 16384, 768], P(None, ('dp', 'tensor')), may hold values from -6 to 6
- gain_attn: float32 [768], replicated, may hold values from 0.1 to 1.9
- gain_mlp: float32 [768], replicated, may hold values from 0.1 to 1.9
- w_qkv: bfloat16 [768, 3, 768], P('dp', None, 'tensor'), may hold values from -0.21875 to 0.21875
- w_out: bfloat16 [768, 768], P('tensor', 'dp'), may hold values from -1.75 to 1.75
- w_up: bfloat16 [768, 3072], P('dp', 'tensor'), may hold values from -0.21875 to 0.21875
- w_down: bfloat16 [3072, 768], P('tensor', 'dp'), may hold values from -0.109375 to 0.109375
- mix_weights: float32 [5], replicated, may hold values from 0.3 to 1.2
- lengths: int32 [16, 4], P('dp'), may hold values from 0 to 1024, as said below
- slot_perm: int32 [16384], P('dp'), may hold values from 0 to 2047, as said below
- grad_out: bfloat16 [16384, 768], P(('dp', 'tensor')), may hold values from -6 to 6
Outputs:
- mixed_out: bfloat16 [16384, 768], P(('dp', 'tensor'))
- grad_hidden: bfloat16 [16384, 768], P(('dp', 'tensor'))
- grad_earlier: bfloat16 [4, 16384, 768], P(None, ('dp', 'tensor'))
- grad_gain_attn: float32 [768], replicated
- grad_gain_mlp: float32 [768], replicated
- grad_w_qkv: float32 [768, 3, 768], P('dp', None, 'tensor')
- grad_w_out: float32 [768, 768], P('tensor', 'dp')
- grad_w_up: float32 [768, 3072], P('dp', 'tensor')
- grad_w_down: float32 [3072, 768], P('tensor', 'dp')
- grad_mix: float32 [5], replicated
The draws below stay inside these ranges and needn't reach their ends.
Inputs may be any that keep to these rules, and one draw needn't show every extreme that they name: Each slot's lengths sum to at most 1024; in every draw some slot holds one sequence of exactly 1024 and entries of 0 there. `slot_perm`: each aligned block of 2048 entries holds every number of 0 to 2047 once.
All inputs are finite; a program needn't handle non-finite values.
Results may differ from the reference program's by a relative error of at most 0.013.
The reference program's roundings to bfloat16 on the way count: a program that leaves them out, or rounds other values in their place, can miss the bound.
Values may be sent and summed in bfloat16 or wider, within the bound.
No kernel may reach another device: no remote copies, remote signals or barrier semaphores. Data moves between devices by JAX's collectives and lax.ppermute only.
A program may use at most 192 MiB of HBM per device.

```python
import jax
import jax.numpy as jnp
from jax import lax

D = 768
HEAD_TOTAL = 12
HEAD_SIZE = 64
FF = 3072
SLOT_LENGTH = 1024
SEGMENT_COUNT = 4
GROUP = 2048
SLOT_TOTAL = 16
TOKENS = 16384


def draw_lengths(key, part):
    selection_random_key = jax.random.fold_in(key, 11)
    primary_random_key = jax.random.fold_in(key, 12)
    remaining_random_key = jax.random.fold_in(key, 13)
    leading_extent = jax.random.randint(primary_random_key, (SLOT_TOTAL, 1), SLOT_LENGTH // 4, SLOT_LENGTH // 2 + 1)
    trailing_extent = jax.random.randint(remaining_random_key, (SLOT_TOTAL, SEGMENT_COUNT - 1), 1, SLOT_LENGTH // (2 * (SEGMENT_COUNT - 1)) + 1)
    ragged = jnp.concatenate([leading_extent, trailing_extent], axis=1).astype(jnp.int32)
    selected_entry = jax.random.randint(selection_random_key, (), 0, SLOT_TOTAL)
    single = jnp.concatenate([jnp.full((1,), SLOT_LENGTH, jnp.int32), jnp.zeros((SEGMENT_COUNT - 1,), jnp.int32)])
    slot_row_block = jnp.arange(SLOT_TOTAL)[:, None]
    return jnp.where(slot_row_block == selected_entry, single[None, :], ragged).astype(jnp.int32)


def draw_slot_perm(key, part):
    block_keys = jax.random.split(jax.random.fold_in(key, 21), TOKENS // GROUP)
    shuffled = jax.vmap(lambda block_key: jax.random.permutation(block_key, GROUP))(block_keys)
    return shuffled.reshape(-1).astype(jnp.int32)


def levels(key, dims, pieces, least, largest):
    def one(axis_at, parts):
        steps = jax.random.uniform(jax.random.fold_in(jax.random.fold_in(key, 6), axis_at), (parts,), jnp.float32, least / len(pieces), largest / len(pieces))
        return jnp.repeat(jnp.exp(steps), dims[axis_at] // parts).reshape((-1,) + (1,) * (len(dims) - axis_at - 1))

    factor_of = one(*pieces[0])
    for cut in pieces[1:]:
        factor_of = factor_of * one(*cut)
    return factor_of


def normal_values(stream_key, shape, scale, limit, cuts=(), kind=jnp.bfloat16):
    loudness = levels(stream_key, shape, cuts, -0.22, 0.18) if cuts else 1.0
    values = jax.random.normal(stream_key, shape, jnp.float32) * scale * loudness
    return jnp.minimum(jnp.maximum(values, -limit), limit).astype(kind)


def setup_inputs(seed: int = 0) -> dict:
    seeds = jax.random.split(jax.random.key(seed), 13)
    return {
        "hidden_in": normal_values(seeds[0], (TOKENS, D), 1.0, 6.0, ((0, 32),)),
        "earlier": normal_values(seeds[1], (4, TOKENS, D), 1.0, 6.0, ((1, 32),)),
        "gain_attn": jnp.clip(1.0 + 0.18 * jax.random.normal(seeds[2], (D,), jnp.float32), 0.1, 1.9),
        "gain_mlp": jnp.clip(1.0 + 0.18 * jax.random.normal(seeds[3], (D,), jnp.float32), 0.1, 1.9),
        "w_qkv": normal_values(seeds[4], (D, 3, D), D ** -0.5, 0.21875, ((0, 8), (2, 4))),
        "w_out": normal_values(seeds[5], (D, D), (D // 64) ** -0.5, 1.75, ((0, 4), (1, 8))),
        "w_up": normal_values(seeds[6], (D, FF), D ** -0.5, 0.21875, ((0, 8), (1, 4))),
        "w_down": normal_values(seeds[7], (FF, D), FF ** -0.5, 0.109375, ((0, 4), (1, 8))),
        "mix_weights": jnp.clip(jax.random.uniform(seeds[8], (5,), jnp.float32, 0.3, 1.2), 0.3, 1.2),
        "lengths": draw_lengths(jax.random.fold_in(seeds[12], 71), 0),
        "slot_perm": draw_slot_perm(jax.random.fold_in(seeds[12], 71), 0),
        "grad_out": normal_values(seeds[11], (TOKENS, D), 1.0, 6.0, ((0, 32),)),
    }


@jax.custom_vjp
def low(v):
    return lax.optimization_barrier(v.astype(jnp.bfloat16)).astype(jnp.float32)

@jax.custom_vjp
def low_back(v):
    return v

def low_keep(v):
    return (low(v), None)

def low_pass(kept, grad):
    return (grad,)

def back_keep(v):
    return (v, None)

def back_low(kept, grad):
    return (low(grad),)
low.defvjp(low_keep, low_pass)
low_back.defvjp(back_keep, back_low)

def layer_norm(value, gain):
    row_mean = lax.optimization_barrier(jnp.mean(value, axis=-1, keepdims=True))
    centered = value - row_mean
    spread = lax.optimization_barrier(jnp.mean(centered * centered, axis=-1, keepdims=True))
    return centered * lax.rsqrt(spread + 1e-05) * gain

def slot_layout(lengths):
    ends = jnp.cumsum(lengths, axis=-1).astype(jnp.int32)
    starts = (ends - lengths).astype(jnp.int32)
    places = jnp.arange(SLOT_LENGTH, dtype=jnp.int32)
    segment = lax.optimization_barrier(jnp.sum((places[None, :, None] >= ends[:, None, :]).astype(jnp.int32), axis=-1))
    begins = jnp.concatenate([starts, ends[:, -1:]], axis=1)
    first = jnp.take_along_axis(begins, segment, axis=1)
    return (segment, places[None, :] - first)

def rotate(value, position):
    half_width = HEAD_SIZE // 2
    inverse = 1.0 / 10000.0 ** (jnp.arange(half_width, dtype=jnp.float32) * (2.0 / HEAD_SIZE))
    phase_angle = position.astype(jnp.float32)[:, None] * inverse[None, :]
    cosine = jnp.cos(phase_angle)[:, None, :]
    sine = jnp.sin(phase_angle)[:, None, :]
    first = value[..., :half_width]
    second = value[..., half_width:]
    return jnp.concatenate([first * cosine - second * sine, second * cosine + first * sine], axis=-1)

def attend(query, key_rows, value_rows, segment):
    scores = jnp.einsum('qhd,khd->hqk', query, key_rows, precision=lax.Precision.HIGHEST) * HEAD_SIZE ** (-0.5)
    scores = low_back(scores)
    places = jnp.arange(SLOT_LENGTH, dtype=jnp.int32)
    allowed = (segment[:, None] == segment[None, :]) & (places[:, None] >= places[None, :])
    scores = jnp.where(allowed[None], scores, -1e+30)
    row_max = lax.optimization_barrier(jnp.max(scores, axis=-1, keepdims=True))
    weights = jnp.exp(scores - row_max)
    probs = low(weights / lax.optimization_barrier(jnp.sum(weights, axis=-1, keepdims=True)))
    return jnp.einsum('hqk,khd->qhd', probs, value_rows, precision=lax.Precision.HIGHEST)

def reference(hidden_in, earlier, gain_attn, gain_mlp, w_qkv, w_out, w_up, w_down, mix_weights, lengths, slot_perm, grad_out):
    segment, position = slot_layout(lengths)
    position = position.reshape(-1)
    base_rows = jnp.arange(TOKENS, dtype=jnp.int32) // GROUP * GROUP
    forward_index = (base_rows + slot_perm).astype(jnp.int32)
    backward_index = jnp.zeros((TOKENS,), jnp.int32).at[forward_index].set(jnp.arange(TOKENS, dtype=jnp.int32))
    attend_block = jax.checkpoint(attend)
    highest = lax.Precision.HIGHEST

    def forward(hidden, prior, g_attn, g_mlp, wq, wo, wu, wd, mixing):
        x_rows = hidden[forward_index]
        normed_attn = low(layer_norm(x_rows, g_attn))
        qkv = low_back(jnp.einsum('rd,dcf->rcf', normed_attn, wq, precision=highest))
        query = low(rotate(qkv[:, 0].reshape(TOKENS, HEAD_TOTAL, HEAD_SIZE), position))
        key_rows = low(rotate(qkv[:, 1].reshape(TOKENS, HEAD_TOTAL, HEAD_SIZE), position))
        value_rows = low(qkv[:, 2].reshape(TOKENS, HEAD_TOTAL, HEAD_SIZE))
        reshape_into_slots = (SLOT_TOTAL, SLOT_LENGTH, HEAD_TOTAL, HEAD_SIZE)
        attended = lax.map(lambda packed: attend_block(*packed), (query.reshape(reshape_into_slots), key_rows.reshape(reshape_into_slots), value_rows.reshape(reshape_into_slots), segment))
        attended = low(low_back(attended.reshape(TOKENS, D)))
        after_attn = x_rows + low_back(jnp.dot(attended, wo, precision=highest))
        normed_mlp = low(layer_norm(after_attn, g_mlp))
        pre_act = low_back(jnp.dot(normed_mlp, wu, precision=highest))
        activated = low(jax.nn.gelu(pre_act, approximate=True))
        block_out = after_attn + low_back(jnp.dot(activated, wd, precision=highest))
        block_out = block_out[backward_index]
        return jnp.einsum('j,jrd->rd', mixing[:4], prior, precision=highest) + mixing[4] * block_out
    primals = (hidden_in.astype(jnp.float32), earlier.astype(jnp.float32), gain_attn, gain_mlp, w_qkv.astype(jnp.float32), w_out.astype(jnp.float32), w_up.astype(jnp.float32), w_down.astype(jnp.float32), mix_weights)
    result, pullback = jax.vjp(forward, *primals)
    grads = pullback(grad_out.astype(jnp.float32))
    return (result.astype(jnp.bfloat16), grads[0].astype(jnp.bfloat16), grads[1].astype(jnp.bfloat16), grads[2], grads[3], grads[4], grads[5], grads[6], grads[7], grads[8])
```

```python
import jax
import jax.numpy as jnp
from jax import lax
from jax.experimental import pallas as pl
from jax.experimental.pallas import tpu as pltpu
from jax.sharding import PartitionSpec as P

HEAD_SIZE = 64
HALF = HEAD_SIZE // 2
LANES = 128
LOG2E = 1.4426950408889634
ROW_STEP = 256

eps = 1e-05
bf16 = jnp.bfloat16
f32 = jnp.float32


def layer_norm(value, gain):
    row_mean = jnp.mean(value, axis=-1, keepdims=True)
    centered = value - row_mean
    spread = jnp.mean(centered * centered, axis=-1, keepdims=True)
    return centered * lax.rsqrt(spread + eps) * gain


def slot_layout(lengths, slot_len):
    ends = jnp.cumsum(lengths, axis=-1)
    places = jnp.arange(slot_len, dtype=jnp.int32)
    passed = places[None, :, None] >= ends[:, None, :]
    first = jnp.max(jnp.where(passed, ends[:, None, :], 0), axis=-1)
    return (first, places[None, :] - first)


def angle_tables(position):
    inverse = 1.0 / 10000.0 ** (jnp.arange(HALF, dtype=f32) * (2.0 / HEAD_SIZE))
    phase_angle = position.astype(f32)[:, None] * inverse[None, :]
    cosine = jnp.cos(phase_angle)
    sine = jnp.sin(phase_angle)
    repeat = LANES // HEAD_SIZE
    return (
        jnp.concatenate([cosine, cosine] * repeat, axis=1),
        jnp.concatenate([-sine, sine] * repeat, axis=1),
    )


def swap_halves(value):
    lane = lax.broadcasted_iota(jnp.int32, value.shape, 1)
    low = (lane % HEAD_SIZE) < HALF
    return jnp.where(low, pltpu.roll(value, LANES - HALF, 1), pltpu.roll(value, HALF, 1))


def turn(value, cosine, sine):
    return value * cosine + swap_halves(value) * sine


def dot(a, b, dims=((1,), (0,))):
    return lax.dot_general(a, b, (dims, ((), ())), preferred_element_type=f32)


def project_kernel(n0, n1, n2, n3, perm_ref, w_ref, cos_ref, sin_ref, slot_ref, qkv_ref):
    pieces = (n0, n1, n2, n3)
    rows = perm_ref.shape[0]
    each = n0.shape[0]
    wanted = perm_ref[...]
    total = None
    for k in range(4):
        here = lax.broadcasted_iota(jnp.int32, (rows, each), 1) + k * each
        pick = jnp.where(here == wanted, 1.0, 0.0).astype(bf16)
        part = dot(pick, pieces[k][...])
        total = part if total is None else total + part
    normed = total.astype(bf16)
    slot_ref[...] = normed
    qkv = dot(normed, w_ref[...])
    cosine = cos_ref[...]
    sine = sin_ref[...]
    third = qkv.shape[1] // 3
    for start in range(0, 2 * third, LANES):
        qkv_ref[:, start : start + LANES] = turn(
            qkv[:, start : start + LANES], cosine, sine
        ).astype(bf16)
    qkv_ref[:, 2 * third :] = qkv[:, 2 * third :].astype(bf16)


def project(pieces, perm_col, w, cosine, sine):
    each, width = pieces[0].shape
    rows = perm_col.shape[0]
    cols = w.shape[1]
    whole = pl.BlockSpec((each, width), lambda i: (0, 0))
    return pl.pallas_call(
        project_kernel,
        grid=(rows // ROW_STEP,),
        in_specs=[whole] * 4
        + [
            pl.BlockSpec((ROW_STEP, 1), lambda i: (i, 0)),
            pl.BlockSpec(w.shape, lambda i: (0, 0)),
            pl.BlockSpec((ROW_STEP, LANES), lambda i: (i, 0)),
            pl.BlockSpec((ROW_STEP, LANES), lambda i: (i, 0)),
        ],
        out_specs=[
            pl.BlockSpec((ROW_STEP, width), lambda i: (i, 0)),
            pl.BlockSpec((ROW_STEP, cols), lambda i: (i, 0)),
        ],
        out_shape=[
            jax.ShapeDtypeStruct((rows, width), bf16),
            jax.ShapeDtypeStruct((rows, cols), bf16),
        ],
        name="project",
    )(*pieces, perm_col, w, cosine, sine)


def spread_rows(perm_ref, value, start, count):
    total = value.shape[0]
    here = lax.broadcasted_iota(jnp.int32, (count, total), 0) + start
    pick = jnp.where(here == perm_ref[...], 1.0, 0.0).astype(bf16)
    return dot(pick, value)


def masked(scores, first_row, query_start):
    key = lax.broadcasted_iota(jnp.int32, scores.shape, 0)
    query = lax.broadcasted_iota(jnp.int32, scores.shape, 1) + query_start
    return jnp.where((key >= first_row) & (key <= query), scores, -1e30)


def attend_kernel(qkv_ref, first_ref, perm_ref, o0, o1, o2, o3, stat_ref, o_all):
    slot = pl.program_id(0)
    length, cols = qkv_ref.shape
    third = cols // 3
    factor = HEAD_SIZE ** (-0.5) * LOG2E
    for head in range(third // HEAD_SIZE):
        at = head * HEAD_SIZE
        key = qkv_ref[:, third + at : third + at + HEAD_SIZE]
        value = qkv_ref[:, 2 * third + at : 2 * third + at + HEAD_SIZE]
        value_t = value.T
        for start in range(0, length, ROW_STEP):
            seen = start + ROW_STEP
            query = qkv_ref[start:seen, at : at + HEAD_SIZE]
            scores = dot(key[:seen], query, ((1,), (1,)))
            scores = masked(scores, first_ref[0, :, start:seen], start)
            top = jnp.max(scores, axis=0, keepdims=True)
            weights = jnp.exp2((scores - top) * factor)
            mass = jnp.sum(weights, axis=0, keepdims=True)
            probs = (weights * (1.0 / mass)).astype(bf16)
            out = dot(value_t[:, :seen], probs).T
            stat_ref[0, head : head + 1, start:seen] = top * factor + jnp.log2(mass)
            o_all[pl.ds(slot * length + start, ROW_STEP), at : at + HEAD_SIZE] = out.astype(bf16)

    @pl.when(slot == pl.num_programs(0) - 1)
    def _():
        each = o0.shape[0]
        for k, ref in enumerate((o0, o1, o2, o3)):
            ref[...] = spread_rows(perm_ref, o_all[...], k * each, each).astype(bf16)


def attend(qkv, first, perm_row, each):
    slots, _, length = first.shape
    rows, cols = qkv.shape
    third = cols // 3
    piece = pl.BlockSpec((each, third), lambda i: (0, 0))
    return pl.pallas_call(
        attend_kernel,
        grid=(slots,),
        in_specs=[
            pl.BlockSpec((length, cols), lambda i: (i, 0)),
            pl.BlockSpec((1, 1, length), lambda i: (i, 0, 0)),
            pl.BlockSpec((1, rows), lambda i: (0, 0)),
        ],
        out_specs=[piece] * 4 + [pl.BlockSpec((1, 8, length), lambda i: (i, 0, 0))],
        out_shape=[jax.ShapeDtypeStruct((each, third), bf16)] * 4
        + [jax.ShapeDtypeStruct((slots, 8, length), f32)],
        scratch_shapes=[pltpu.VMEM((rows, third), bf16)],
        name="attend",
    )(qkv, first, perm_row)


def attend_back_kernel(
    qkv_ref, first_ref, perm_ref, d0, d1, d2, d3, stat_ref, cos_ref, sin_ref, out_ref, acc, given
):
    length, cols = qkv_ref.shape
    third = cols // 3
    scale = HEAD_SIZE ** (-0.5)
    factor = scale * LOG2E
    each = d0.shape[0]
    for start in range(0, length, ROW_STEP):
        total = None
        for k, ref in enumerate((d0, d1, d2, d3)):
            here = lax.broadcasted_iota(jnp.int32, (ROW_STEP, each), 1) + k * each
            pick = jnp.where(here == perm_ref[start : start + ROW_STEP, :], 1.0, 0.0).astype(bf16)
            part = dot(pick, ref[...])
            total = part if total is None else total + part
        given[start : start + ROW_STEP, :] = total.astype(bf16)
    acc[:, third:] = jnp.zeros((length, 2 * third), f32)
    for head in range(third // HEAD_SIZE):
        at = head * HEAD_SIZE
        key = qkv_ref[:, third + at : third + at + HEAD_SIZE]
        value = qkv_ref[:, 2 * third + at : 2 * third + at + HEAD_SIZE]
        key_t = key.T
        for start in range(0, length, ROW_STEP):
            seen = start + ROW_STEP
            query = qkv_ref[start:seen, at : at + HEAD_SIZE]
            grad = given[start:seen, at : at + HEAD_SIZE]
            scores = dot(key[:seen], query, ((1,), (1,)))
            scores = masked(scores, first_ref[0, :, start:seen], start)
            probs = jnp.exp2(scores * factor - stat_ref[0, head : head + 1, start:seen])
            grad_probs = dot(value[:seen], grad, ((1,), (1,)))
            delta = jnp.sum(probs * grad_probs, axis=0, keepdims=True)
            grad_scores = (probs * (grad_probs - delta)).astype(bf16)
            acc[start:seen, at : at + HEAD_SIZE] = dot(key_t[:, :seen], grad_scores).T
            acc[:seen, third + at : third + at + HEAD_SIZE] += dot(grad_scores, query)
            acc[:seen, 2 * third + at : 2 * third + at + HEAD_SIZE] += dot(
                probs.astype(bf16), grad
            )
    cosine = cos_ref[...]
    sine = -sin_ref[...]
    for start in range(0, 2 * third, LANES):
        out_ref[:, start : start + LANES] = turn(
            acc[:, start : start + LANES] * scale, cosine, sine
        ).astype(bf16)
    out_ref[:, 2 * third :] = acc[:, 2 * third :].astype(bf16)


def attend_back(qkv, first, perm_col, grads, stat, cosine, sine):
    slots, _, length = first.shape
    rows, cols = qkv.shape
    third = cols // 3
    piece = pl.BlockSpec(grads[0].shape, lambda i: (0, 0))
    return pl.pallas_call(
        attend_back_kernel,
        grid=(slots,),
        in_specs=[
            pl.BlockSpec((length, cols), lambda i: (i, 0)),
            pl.BlockSpec((1, 1, length), lambda i: (i, 0, 0)),
            pl.BlockSpec((length, 1), lambda i: (i, 0)),
        ]
        + [piece] * 4
        + [
            pl.BlockSpec((1, 8, length), lambda i: (i, 0, 0)),
            pl.BlockSpec((length, LANES), lambda i: (i, 0)),
            pl.BlockSpec((length, LANES), lambda i: (i, 0)),
        ],
        out_specs=pl.BlockSpec((length, cols), lambda i: (i, 0)),
        out_shape=jax.ShapeDtypeStruct((rows, cols), bf16),
        scratch_shapes=[pltpu.VMEM((length, cols), f32), pltpu.VMEM((length, third), bf16)],
        name="attend_back",
    )(qkv, first, perm_col, *grads, stat, cosine, sine)


def unproject(dqkv, perm_row, w, each):
    rows, cols = dqkv.shape
    width = w.shape[0]

    def kernel(dqkv_ref, perm_ref, w_ref, out_ref):
        start = pl.program_id(0) * ROW_STEP
        picked = spread_rows(perm_ref, dqkv_ref[...], start, ROW_STEP).astype(bf16)
        out_ref[...] = dot(picked, w_ref[...], ((1,), (1,))).astype(bf16)

    return pl.pallas_call(
        kernel,
        grid=(rows // ROW_STEP,),
        in_specs=[
            pl.BlockSpec((rows, cols), lambda i: (0, 0)),
            pl.BlockSpec((1, rows), lambda i: (0, 0)),
            pl.BlockSpec(w.shape, lambda i: (0, 0)),
        ],
        out_specs=pl.BlockSpec((ROW_STEP, width), lambda i: (i, 0)),
        out_shape=jax.ShapeDtypeStruct((rows, width), bf16),
        name="unproject",
    )(dqkv, perm_row, w)


def hop(value, axis, bit):
    count = lax.axis_size(axis)
    return lax.ppermute(value, axis, [(i, i ^ bit) for i in range(count)])


def gather_tensor(value):
    far = hop(value, "tensor", 2)
    near = hop(value, "tensor", 1)
    cross = hop(far, "tensor", 1)
    return [value, near, far, cross]


def exchange_tensor(pieces):
    return [pieces[0]] + [hop(pieces[k], "tensor", k) for k in (1, 2, 3)]


def scatter_tensor(pieces):
    over = hop(pieces[3].astype(bf16), "tensor", 1)
    beside = hop(pieces[1].astype(bf16), "tensor", 1)
    outward = (pieces[2].astype(f32) + over.astype(f32)).astype(bf16)
    back = hop(outward, "tensor", 2)
    return pieces[0].astype(f32) + beside.astype(f32) + back.astype(f32)


def total_all(value):
    for axis in ("tensor", "dp"):
        bit = 1
        while bit < lax.axis_size(axis):
            value = value + hop(value, axis, bit)
            bit *= 2
    return value


def gather_dp(value):
    return lax.all_gather(value, "dp", axis=0, tiled=True)


def scatter_dp(value):
    return lax.psum_scatter(value.astype(bf16), "dp", scatter_dimension=0, tiled=True).astype(f32)


def gelu_tanh(pre_value):
    return jax.nn.gelu(pre_value, approximate=True)


def local(
    hidden_in,
    earlier,
    gain_attn,
    gain_mlp,
    w_qkv,
    w_out,
    w_up,
    w_down,
    mix_weights,
    lengths,
    slot_perm,
    grad_out,
):
    tensor_place = lax.axis_index("tensor")
    own_rows, width = hidden_in.shape
    slot_count = lengths.shape[0]
    group_rows = slot_perm.shape[0]
    slot_len = group_rows // slot_count
    shard_d = w_qkv.shape[0]
    head_cols = w_qkv.shape[2]

    hidden = hidden_in.astype(f32)
    normed_attn = layer_norm(hidden, gain_attn).astype(bf16)
    attn_pieces = gather_tensor(normed_attn)
    full_qkv = gather_dp(w_qkv.reshape(shard_d, 3 * head_cols))
    out_pieces = gather_tensor(w_out.T)
    full_out = gather_dp(jnp.concatenate(out_pieces, axis=1))
    full_up = gather_dp(w_up)
    full_down_t = gather_dp(w_down.T)

    first, position = slot_layout(lengths, slot_len)
    first = first.reshape(slot_count, 1, slot_len)
    cosine, sine = angle_tables(position.reshape(-1))
    perm = ((slot_perm // own_rows) ^ tensor_place) * own_rows + slot_perm % own_rows
    perm_col = perm[:, None]
    perm_row = perm[None, :]

    normed_slot, qkv = project(attn_pieces, perm_col, full_qkv, cosine, sine)
    *attended, stat = attend(qkv, first, perm_row, own_rows)
    heads_here = jnp.concatenate(exchange_tensor(attended), axis=1)
    after_attn = hidden + dot(heads_here, full_out, ((1,), (1,)))
    normed_mlp = layer_norm(after_attn, gain_mlp).astype(bf16)
    mlp_rows = jnp.concatenate(gather_tensor(normed_mlp), axis=0)

    cotangent = grad_out.astype(f32)
    own_grad = mix_weights[4] * cotangent
    grad_rows = jnp.concatenate(gather_tensor(own_grad.astype(bf16)), axis=0)

    pre_act = dot(mlp_rows, full_up)
    activated = gelu_tanh(pre_act).astype(bf16)
    grad_act = dot(grad_rows, full_down_t)
    unused_value, gelu_back = jax.vjp(gelu_tanh, pre_act)
    grad_pre = gelu_back(grad_act)[0].astype(bf16)
    partial = dot(grad_pre, full_up, ((1,), (1,)))
    grad_normed_mlp = scatter_tensor(
        [partial[k * own_rows : (k + 1) * own_rows] for k in range(4)]
    )
    partial_out = dot(activated, full_down_t, ((1,), (1,)))
    block_out = after_attn + scatter_tensor(
        [partial_out[k * own_rows : (k + 1) * own_rows] for k in range(4)]
    )
    grad_down_t = scatter_dp(dot(grad_rows, activated, ((0,), (0,))))
    grad_up = scatter_dp(dot(mlp_rows, grad_pre, ((0,), (0,))))

    unused_norm, second_back = jax.vjp(layer_norm, after_attn, gain_mlp)
    grad_resid_mlp, grad_gain_mlp = second_back(grad_normed_mlp)
    grad_after = own_grad + grad_resid_mlp
    grad_low = grad_after.astype(bf16)
    grad_heads = dot(grad_low, full_out).astype(bf16)
    grad_attended = exchange_tensor(
        [grad_heads[:, k * head_cols : (k + 1) * head_cols] for k in range(4)]
    )
    out_partial = dot(grad_low, heads_here, ((0,), (0,)))
    out_scattered = scatter_tensor(
        [out_partial[:, k * head_cols : (k + 1) * head_cols] for k in range(4)]
    )
    grad_out_t = scatter_dp(out_scattered)

    dqkv = attend_back(qkv, first, perm_col, grad_attended, stat, cosine, sine)
    attn_partial = unproject(dqkv, perm_row, full_qkv, own_rows)
    grad_normed_attn = scatter_tensor(
        [attn_partial[k * own_rows : (k + 1) * own_rows] for k in range(4)]
    )
    qkv_partial = dot(normed_slot, dqkv, ((0,), (0,)))
    grad_qkv = scatter_dp(qkv_partial)
    grad_gain_attn = jnp.sum(qkv_partial * full_qkv.astype(f32), axis=1) / gain_attn

    unused_first, first_back = jax.vjp(lambda value: layer_norm(value, gain_attn), hidden)
    grad_hidden = (grad_after + first_back(grad_normed_attn)[0]).astype(bf16)

    prior = [earlier[index].astype(f32) for index in range(4)]
    mixed_total = mix_weights[4] * block_out
    for index in range(4):
        mixed_total = mixed_total + mix_weights[index] * prior[index]
    grad_earlier = (mix_weights[:4, None, None] * cotangent[None]).astype(bf16)
    mix_terms = [jnp.sum(cotangent * value) for value in prior + [block_out]]
    spare = -(2 * width + 5) % 1024
    packed = jnp.concatenate(
        [grad_gain_attn, grad_gain_mlp, jnp.stack(mix_terms), jnp.zeros((spare,), f32)]
    )
    packed = total_all(packed.reshape(-1, LANES)).reshape(-1)
    return (
        mixed_total.astype(bf16),
        grad_hidden,
        grad_earlier,
        packed[:width],
        packed[width : 2 * width],
        grad_qkv.reshape(shard_d, 3, head_cols),
        grad_out_t.T,
        grad_up,
        grad_down_t.T,
        packed[2 * width : 2 * width + 5],
    )


def solution(mesh):
    rows = P(("dp", "tensor"), None)
    layers = P(None, ("dp", "tensor"), None)
    return jax.shard_map(
        local,
        mesh=mesh,
        in_specs=(
            rows,
            layers,
            P(),
            P(),
            P("dp", None, "tensor"),
            P("tensor", "dp"),
            P("dp", "tensor"),
            P("tensor", "dp"),
            P(),
            P("dp", None),
            P("dp"),
            rows,
        ),
        out_specs=(
            rows,
            rows,
            layers,
            P(),
            P(),
            P("dp", None, "tensor"),
            P("tensor", "dp"),
            P("dp", "tensor"),
            P("tensor", "dp"),
            P(),
        ),
        check_vma=False,
    )
```

```python
import jax
import jax.numpy as jnp
from jax import lax
from jax.experimental import pallas as pl
from jax.experimental.pallas import tpu as pltpu
from jax.sharding import PartitionSpec as P


HEAD_SIZE = 64
HALF = HEAD_SIZE // 2
LANES = 128
LOG2E = 1.4426950408889634
ROW_STEP = 256

eps = 1e-05
bf16 = jnp.bfloat16
f32 = jnp.float32


def layer_norm(value, gain):
    row_mean = jnp.mean(value, axis=-1, keepdims=True)
    centered = value - row_mean
    spread = jnp.mean(centered * centered, axis=-1, keepdims=True)
    return centered * lax.rsqrt(spread + eps) * gain


def slot_layout(lengths, slot_len):
    ends = jnp.cumsum(lengths, axis=-1)
    places = jnp.arange(slot_len, dtype=jnp.int32)
    passed = places[None, :, None] >= ends[:, None, :]
    first = jnp.max(jnp.where(passed, ends[:, None, :], 0), axis=-1)
    return (first, places[None, :] - first)


def angle_tables(position):
    inverse = 1.0 / 10000.0 ** (jnp.arange(HALF, dtype=f32) * (2.0 / HEAD_SIZE))
    phase_angle = position.astype(f32)[:, None] * inverse[None, :]
    cosine = jnp.cos(phase_angle)
    sine = jnp.sin(phase_angle)
    repeat = LANES // HEAD_SIZE
    return (
        jnp.concatenate([cosine, cosine] * repeat, axis=1),
        jnp.concatenate([-sine, sine] * repeat, axis=1),
    )


def swap_halves(value):
    lane = lax.broadcasted_iota(jnp.int32, value.shape, 1)
    low = (lane % HEAD_SIZE) < HALF
    return jnp.where(low, pltpu.roll(value, LANES - HALF, 1), pltpu.roll(value, HALF, 1))


def turn(value, cosine, sine):
    return value * cosine + swap_halves(value) * sine


def dot(a, b, dims=((1,), (0,))):
    return lax.dot_general(a, b, (dims, ((), ())), preferred_element_type=f32)


def order_kernel(n0, n1, n2, n3, perm_ref, slot_ref):
    slot_ref[...] = pick_rows(perm_ref[...], (n0, n1, n2, n3)).astype(bf16)


def pick_rows(wanted, pieces):
    each = pieces[0].shape[0]
    total = None
    for k in range(4):
        here = lax.broadcasted_iota(jnp.int32, (wanted.shape[0], each), 1) + k * each
        pick = jnp.where(here == wanted, 1.0, 0.0).astype(bf16)
        part = dot(pick, pieces[k][...])
        total = part if total is None else total + part
    return total


def to_slots(pieces, perm_col):
    each, width = pieces[0].shape
    rows = perm_col.shape[0]
    whole = pl.BlockSpec((each, width), lambda i: (0, 0))
    return pl.pallas_call(
        order_kernel,
        grid=(rows // ROW_STEP,),
        in_specs=[whole] * 4 + [pl.BlockSpec((ROW_STEP, 1), lambda i: (i, 0))],
        out_specs=pl.BlockSpec((ROW_STEP, width), lambda i: (i, 0)),
        out_shape=jax.ShapeDtypeStruct((rows, width), bf16),
        name="to_slots",
    )(*pieces, perm_col)


def project_kernel(normed_ref, w_ref, cos_ref, sin_ref, qkv_ref):
    qkv = dot(normed_ref[...], w_ref[...])
    cosine = cos_ref[...]
    sine = sin_ref[...]
    third = qkv.shape[1] // 3
    for start in range(0, 2 * third, LANES):
        qkv_ref[:, start : start + LANES] = turn(
            qkv[:, start : start + LANES], cosine, sine
        ).astype(bf16)
    qkv_ref[:, 2 * third :] = qkv[:, 2 * third :].astype(bf16)


def project(normed, w, cosine, sine):
    rows, width = normed.shape
    cols = w.shape[1]
    step = 2 * ROW_STEP
    return pl.pallas_call(
        project_kernel,
        grid=(rows // step,),
        in_specs=[
            pl.BlockSpec((step, width), lambda i: (i, 0)),
            pl.BlockSpec(w.shape, lambda i: (0, 0)),
            pl.BlockSpec((step, LANES), lambda i: (i, 0)),
            pl.BlockSpec((step, LANES), lambda i: (i, 0)),
        ],
        out_specs=pl.BlockSpec((step, cols), lambda i: (i, 0)),
        out_shape=jax.ShapeDtypeStruct((rows, cols), bf16),
        name="project",
    )(normed, w, cosine, sine)


def mlp_kernel(a_ref, b_ref, ga_ref, gb_ref, up_ref, down_ref, *outs):
    c = 0.7978845608028654
    for n, (rows_ref, grad_ref) in enumerate(((a_ref, ga_ref), (b_ref, gb_ref))):
        dn_ref, hid_ref, du_ref = outs[3 * n : 3 * n + 3]
        u = dot(rows_ref[...], up_ref[...])
        square = u * u
        t = jnp.tanh(c * (u * (1.0 + 0.044715 * square)))
        half = 0.5 * (1.0 + t)
        hid_ref[...] = (u * half).astype(bf16)
        slope = half + 0.5 * u * (1.0 - t * t) * (c * (1.0 + 3 * 0.044715 * square))
        du = (dot(grad_ref[...], down_ref[...]) * slope).astype(bf16)
        du_ref[...] = du
        dn_ref[...] = dot(du, up_ref[...], ((1,), (1,))).astype(bf16)


def mlp(rows, grads, updown):
    each, width = rows[0].shape
    units = updown.shape[1] // 2
    block = pl.BlockSpec((ROW_STEP, width), lambda i: (i, 0))
    inner = pl.BlockSpec((ROW_STEP, units), lambda i: (i, 0))
    wide = jax.ShapeDtypeStruct((each, width), bf16)
    mid = jax.ShapeDtypeStruct((each, units), bf16)
    return pl.pallas_call(
        mlp_kernel,
        grid=(each // ROW_STEP,),
        in_specs=[block] * 4
        + [
            pl.BlockSpec((width, units), lambda i: (0, 0)),
            pl.BlockSpec((width, units), lambda i: (0, 1)),
        ],
        out_specs=[block, inner, inner] * 2,
        out_shape=[wide, mid, mid] * 2,
    )(*rows, *grads, updown, updown)


def mlp_out_kernel(h0, h1, h2, h3, down_ref, o0, o1, o2, o3):
    for hid_ref, out_ref in ((h3, o3), (h2, o2), (h1, o1), (h0, o0)):
        out_ref[...] = dot(hid_ref[...], down_ref[...], ((1,), (1,))).astype(bf16)


def mlp_out(hids, updown):
    each, units = hids[0].shape
    width = updown.shape[0]
    return pl.pallas_call(
        mlp_out_kernel,
        grid=(each // ROW_STEP,),
        in_specs=[pl.BlockSpec((ROW_STEP, units), lambda i: (i, 0))] * 4
        + [pl.BlockSpec((width, units), lambda i: (0, 1))],
        out_specs=[pl.BlockSpec((ROW_STEP, width), lambda i: (i, 0))] * 4,
        out_shape=[jax.ShapeDtypeStruct((each, width), bf16)] * 4,
        name="mlp_out",
    )(*hids, updown)


def mlp_weights_kernel(*refs):
    rows, grads, hids, dus = refs[:4], refs[4:8], refs[8:12], refs[12:16]
    out_ref, acc = refs[16:]
    units = hids[0].shape[1]
    step = pl.program_id(0)

    @pl.when(step == 0)
    def _():
        acc[...] = jnp.zeros(acc.shape, f32)

    up = down = None
    for k in range(4):
        a = dot(rows[k][...], dus[k][...], ((0,), (0,)))
        b = dot(grads[k][...], hids[k][...], ((0,), (0,)))
        up = a if up is None else up + a
        down = b if down is None else down + b
    acc[:, :units] += up
    acc[:, units:] += down

    @pl.when(step == pl.num_programs(0) - 1)
    def _():
        out_ref[...] = acc[...].astype(bf16)


def mlp_weights(rows, grads, hids, dus):
    each, width = rows[0].shape
    units = hids[0].shape[1]
    block = pl.BlockSpec((ROW_STEP, width), lambda i: (i, 0))
    inner = pl.BlockSpec((ROW_STEP, units), lambda i: (i, 0))
    return pl.pallas_call(
        mlp_weights_kernel,
        grid=(each // ROW_STEP,),
        in_specs=[block] * 8 + [inner] * 8,
        out_specs=pl.BlockSpec((width, 2 * units), lambda i: (0, 0)),
        out_shape=jax.ShapeDtypeStruct((width, 2 * units), bf16),
        scratch_shapes=[pltpu.VMEM((width, 2 * units), f32)],
        name="mlp_weights",
    )(*rows, *grads, *hids, *dus)


def spread_rows(perm_ref, value, start, count):
    total = value.shape[0]
    here = lax.broadcasted_iota(jnp.int32, (count, total), 0) + start
    pick = jnp.where(here == perm_ref[...], 1.0, 0.0).astype(bf16)
    return dot(pick, value)


def masked(scores, first_row, query_start):
    key = lax.broadcasted_iota(jnp.int32, scores.shape, 0)
    query = lax.broadcasted_iota(jnp.int32, scores.shape, 1) + query_start
    return jnp.where((key >= first_row) & (key <= query), scores, -1e30)


def attend_kernel(qkv_ref, first_ref, perm_ref, o0, o1, o2, o3, stat_ref, o_all):
    slot = pl.program_id(0)
    length, cols = qkv_ref.shape
    third = cols // 3
    factor = HEAD_SIZE ** (-0.5) * LOG2E
    for head in range(third // HEAD_SIZE):
        at = head * HEAD_SIZE
        key = qkv_ref[:, third + at : third + at + HEAD_SIZE]
        value = qkv_ref[:, 2 * third + at : 2 * third + at + HEAD_SIZE]
        value_t = value.T
        for start in range(0, length, ROW_STEP):
            seen = start + ROW_STEP
            query = qkv_ref[start:seen, at : at + HEAD_SIZE]
            scores = dot(key[:seen], query, ((1,), (1,)))
            scores = masked(scores, first_ref[0, :, start:seen], start)
            top = jnp.max(scores, axis=0, keepdims=True)
            weights = jnp.exp2((scores - top) * factor)
            mass = jnp.sum(weights, axis=0, keepdims=True)
            probs = (weights * (1.0 / mass)).astype(bf16)
            out = dot(value_t[:, :seen], probs).T
            stat_ref[0, head : head + 1, start:seen] = top * factor + jnp.log2(mass)
            o_all[pl.ds(slot * length + start, ROW_STEP), at : at + HEAD_SIZE] = out.astype(bf16)

    @pl.when(slot == pl.num_programs(0) - 1)
    def _():
        each = o0.shape[0]
        for k, ref in enumerate((o0, o1, o2, o3)):
            ref[...] = spread_rows(perm_ref, o_all[...], k * each, each).astype(bf16)


def attend(qkv, first, perm_row, each):
    slots, _, length = first.shape
    rows, cols = qkv.shape
    third = cols // 3
    piece = pl.BlockSpec((each, third), lambda i: (0, 0))
    return pl.pallas_call(
        attend_kernel,
        grid=(slots,),
        in_specs=[
            pl.BlockSpec((length, cols), lambda i: (i, 0)),
            pl.BlockSpec((1, 1, length), lambda i: (i, 0, 0)),
            pl.BlockSpec((1, rows), lambda i: (0, 0)),
        ],
        out_specs=[piece] * 4 + [pl.BlockSpec((1, 8, length), lambda i: (i, 0, 0))],
        out_shape=[jax.ShapeDtypeStruct((each, third), bf16)] * 4
        + [jax.ShapeDtypeStruct((slots, 8, length), f32)],
        scratch_shapes=[pltpu.VMEM((rows, third), bf16)],
        name="attend",
    )(qkv, first, perm_row)


def attend_back_kernel(
    qkv_ref, first_ref, perm_ref, d0, d1, d2, d3, stat_ref, cos_ref, sin_ref, out_ref, acc, given
):
    length, cols = qkv_ref.shape
    third = cols // 3
    scale = HEAD_SIZE ** (-0.5)
    factor = scale * LOG2E
    for start in range(0, length, ROW_STEP):
        wanted = perm_ref[start : start + ROW_STEP, :]
        given[start : start + ROW_STEP, :] = pick_rows(wanted, (d0, d1, d2, d3)).astype(bf16)
    acc[:, third:] = jnp.zeros((length, 2 * third), f32)
    for head in range(third // HEAD_SIZE):
        at = head * HEAD_SIZE
        key = qkv_ref[:, third + at : third + at + HEAD_SIZE]
        value = qkv_ref[:, 2 * third + at : 2 * third + at + HEAD_SIZE]
        key_t = key.T
        for start in range(0, length, ROW_STEP):
            seen = start + ROW_STEP
            query = qkv_ref[start:seen, at : at + HEAD_SIZE]
            grad = given[start:seen, at : at + HEAD_SIZE]
            scores = dot(key[:seen], query, ((1,), (1,)))
            scores = masked(scores, first_ref[0, :, start:seen], start)
            probs = jnp.exp2(scores * factor - stat_ref[0, head : head + 1, start:seen])
            grad_probs = dot(value[:seen], grad, ((1,), (1,)))
            delta = jnp.sum(probs * grad_probs, axis=0, keepdims=True)
            grad_scores = (probs * (grad_probs - delta)).astype(bf16)
            acc[start:seen, at : at + HEAD_SIZE] = dot(key_t[:, :seen], grad_scores).T
            acc[:seen, third + at : third + at + HEAD_SIZE] += dot(grad_scores, query)
            acc[:seen, 2 * third + at : 2 * third + at + HEAD_SIZE] += dot(
                probs.astype(bf16), grad
            )
    cosine = cos_ref[...]
    sine = -sin_ref[...]
    for start in range(0, 2 * third, LANES):
        out_ref[:, start : start + LANES] = turn(
            acc[:, start : start + LANES] * scale, cosine, sine
        ).astype(bf16)
    out_ref[:, 2 * third :] = acc[:, 2 * third :].astype(bf16)


def attend_back(qkv, first, perm_col, grads, stat, cosine, sine):
    slots, _, length = first.shape
    rows, cols = qkv.shape
    third = cols // 3
    piece = pl.BlockSpec(grads[0].shape, lambda i: (0, 0))
    return pl.pallas_call(
        attend_back_kernel,
        grid=(slots,),
        in_specs=[
            pl.BlockSpec((length, cols), lambda i: (i, 0)),
            pl.BlockSpec((1, 1, length), lambda i: (i, 0, 0)),
            pl.BlockSpec((length, 1), lambda i: (i, 0)),
        ]
        + [piece] * 4
        + [
            pl.BlockSpec((1, 8, length), lambda i: (i, 0, 0)),
            pl.BlockSpec((length, LANES), lambda i: (i, 0)),
            pl.BlockSpec((length, LANES), lambda i: (i, 0)),
        ],
        out_specs=pl.BlockSpec((length, cols), lambda i: (i, 0)),
        out_shape=jax.ShapeDtypeStruct((rows, cols), bf16),
        scratch_shapes=[pltpu.VMEM((length, cols), f32), pltpu.VMEM((length, third), bf16)],
        name="attend_back",
    )(qkv, first, perm_col, *grads, stat, cosine, sine)


def unproject(dqkv, perm_row, w, each, first):
    rows, cols = dqkv.shape
    width = w.shape[0]

    def kernel(dqkv_ref, perm_ref, w_ref, a_ref, b_ref):
        for k, out_ref in ((first + 1, b_ref), (first, a_ref)):
            start = k * each + pl.program_id(0) * ROW_STEP
            picked = spread_rows(perm_ref, dqkv_ref[...], start, ROW_STEP).astype(bf16)
            out_ref[...] = dot(picked, w_ref[...], ((1,), (1,))).astype(bf16)

    return pl.pallas_call(
        kernel,
        grid=(each // ROW_STEP,),
        in_specs=[
            pl.BlockSpec((rows, cols), lambda i: (0, 0)),
            pl.BlockSpec((1, rows), lambda i: (0, 0)),
            pl.BlockSpec(w.shape, lambda i: (0, 0)),
        ],
        out_specs=[pl.BlockSpec((ROW_STEP, width), lambda i: (i, 0))] * 2,
        out_shape=[jax.ShapeDtypeStruct((each, width), bf16)] * 2,
    )(dqkv, perm_row, w)


def hop(value, axis, bit):
    count = lax.axis_size(axis)
    return lax.ppermute(value, axis, [(i, i ^ bit) for i in range(count)])


def gather_tensor(value):
    near = hop(value, "tensor", 1)
    far = hop(value, "tensor", 2)
    cross = hop(far, "tensor", 1)
    return [value, near, far, cross]


def exchange_tensor(pieces):
    out = [pieces[0], hop(pieces[1], "tensor", 1)]
    return out + [hop(pieces[k], "tensor", k) for k in (2, 3)]


def scatter_tensor(pieces):
    over = hop(pieces[3].astype(bf16), "tensor", 1)
    outward = (pieces[2].astype(f32) + over.astype(f32)).astype(bf16)
    back = hop(outward, "tensor", 2)
    beside = hop(pieces[1].astype(bf16), "tensor", 1)
    return pieces[0].astype(f32) + beside.astype(f32) + back.astype(f32)


def total_all(value):
    for axis in ("tensor", "dp"):
        bit = 1
        while bit < lax.axis_size(axis):
            value = value + hop(value, axis, bit)
            bit *= 2
    return value


def gather_dp(value):
    return lax.all_gather(value, "dp", axis=0, tiled=True)


def scatter_dp(value):
    return lax.psum_scatter(value.astype(bf16), "dp", scatter_dimension=0, tiled=True).astype(f32)


def gather_dp_steps(value):
    count = lax.axis_size("dp")
    if count > 8:
        return gather_dp(value)
    place = lax.axis_index("dp")
    share = value.shape
    bit = count // 2
    axis = 0
    while bit:
        other = hop(value, "dp", bit)
        upper = (place & bit) > 0
        low = jnp.where(upper, other, value)
        high = jnp.where(upper, value, other)
        value = jnp.stack([low, high], axis=axis)
        axis += 1
        bit //= 2
    return value.reshape((count * share[0],) + share[1:])


def scatter_dp_parts(parts):
    count = lax.axis_size("dp")
    parts = parts[:1] + [hop(parts[k], "dp", k) for k in range(1, count)]
    total = parts[0].astype(f32)
    for part in parts[1:]:
        total = total + part.astype(f32)
    return total


def qkv_weights_kernel(place_ref, normed_ref, dqkv_ref, w_ref, other_ref, *refs):
    parts, gain_ref, acc = refs[:-2], refs[-2], refs[-1]
    step = pl.program_id(0)
    cols = acc.shape[1]
    part = dot(normed_ref[...], dqkv_ref[...], ((0,), (0,)))

    @pl.when(step == 0)
    def _():
        acc[...] = part

    @pl.when(step > 0)
    def _():
        acc[...] += part

    @pl.when(step == pl.num_programs(0) - 1)
    def _():
        gain_ref[...] = jnp.sum(acc[...] * w_ref[...].astype(f32), axis=1, keepdims=True)
        share = acc.shape[0] // len(parts)
        for k, ref in enumerate(parts):
            at = pl.multiple_of((place_ref[0] ^ k) * share, 8)
            ref[:, :cols] = acc[pl.ds(at, share), :].astype(bf16)
            ref[:, cols:] = other_ref[pl.ds(at, share), :].astype(bf16)


def qkv_weights(normed, dqkv, w, other, place, count):
    rows, width = normed.shape
    cols = dqkv.shape[1]
    extra = other.shape[1]
    step = 2 * ROW_STEP
    share = width // count
    return pl.pallas_call(
        qkv_weights_kernel,
        grid=(rows // step,),
        in_specs=[
            pl.BlockSpec(memory_space=pltpu.SMEM),
            pl.BlockSpec((step, width), lambda i: (i, 0)),
            pl.BlockSpec((step, cols), lambda i: (i, 0)),
            pl.BlockSpec(w.shape, lambda i: (0, 0)),
            pl.BlockSpec(other.shape, lambda i: (0, 0)),
        ],
        out_specs=[pl.BlockSpec((share, cols + extra), lambda i: (0, 0))] * count
        + [pl.BlockSpec((width, 1), lambda i: (0, 0))],
        out_shape=[jax.ShapeDtypeStruct((share, cols + extra), bf16)] * count
        + [jax.ShapeDtypeStruct((width, 1), f32)],
        scratch_shapes=[pltpu.VMEM((width, cols), f32)],
        name="qkv_weights",
    )(place, normed, dqkv, w, other)


def layer(
    hidden_in,
    earlier,
    gain_attn,
    gain_mlp,
    w_qkv,
    w_out,
    w_up,
    w_down,
    mix_weights,
    lengths,
    slot_perm,
    grad_out,
):
    tensor_place = lax.axis_index("tensor")
    own_rows, width = hidden_in.shape
    slot_count = lengths.shape[0]
    group_rows = slot_perm.shape[0]
    slot_len = group_rows // slot_count
    shard_d = w_qkv.shape[0]
    head_cols = w_qkv.shape[2]

    hidden = hidden_in.astype(f32)
    normed_attn = layer_norm(hidden, gain_attn).astype(bf16)
    attn_pieces = gather_tensor(normed_attn)
    full_qkv = gather_dp_steps(w_qkv.reshape(shard_d, 3 * head_cols))
    out_pieces = gather_tensor(w_out.T)
    full_out = gather_dp(jnp.concatenate(out_pieces, axis=1))
    updown = gather_dp(jnp.concatenate([w_up, w_down.T], axis=1))

    first, position = slot_layout(lengths, slot_len)
    first = first.reshape(slot_count, 1, slot_len)
    cosine, sine = angle_tables(position.reshape(-1))
    perm = ((slot_perm // own_rows) ^ tensor_place) * own_rows + slot_perm % own_rows
    perm_col = perm[:, None]
    perm_row = perm[None, :]

    cotangent = grad_out.astype(f32)
    own_grad = mix_weights[4] * cotangent
    grad_pieces = gather_tensor(own_grad.astype(bf16))

    normed_slot = to_slots(attn_pieces, perm_col)
    qkv = project(normed_slot, full_qkv, cosine, sine)
    *attended, stat = attend(qkv, first, perm_row, own_rows)
    heads_here = jnp.concatenate(exchange_tensor(attended), axis=1)
    after_attn = hidden + dot(heads_here, full_out, ((1,), (1,)))
    normed_mlp = layer_norm(after_attn, gain_mlp).astype(bf16)
    mlp_rows = gather_tensor(normed_mlp)

    dn0, hid0, du0, dn1, hid1, du1 = mlp(mlp_rows[:2], grad_pieces[:2], updown)
    dn2, hid2, du2, dn3, hid3, du3 = mlp(mlp_rows[2:], grad_pieces[2:], updown)
    grad_normed_mlp = scatter_tensor([dn0, dn1, dn2, dn3])
    hids = [hid0, hid1, hid2, hid3]
    mlp_total = scatter_tensor(mlp_out(hids, updown))
    grad_updown = scatter_dp(mlp_weights(mlp_rows, grad_pieces, hids, [du0, du1, du2, du3]))
    units = w_up.shape[1]
    grad_up = grad_updown[:, :units]
    grad_down_t = grad_updown[:, units:]

    _, second_back = jax.vjp(layer_norm, after_attn, gain_mlp)
    grad_resid_mlp, grad_gain_mlp = second_back(grad_normed_mlp)
    grad_after = own_grad + grad_resid_mlp
    grad_low = grad_after.astype(bf16)
    grad_heads = dot(grad_low, full_out).astype(bf16)
    grad_attended = exchange_tensor(
        [grad_heads[:, k * head_cols : (k + 1) * head_cols] for k in range(4)]
    )
    out_partial = dot(grad_low, heads_here, ((0,), (0,)))
    out_scattered = scatter_tensor(
        [out_partial[:, k * head_cols : (k + 1) * head_cols] for k in range(4)]
    )
    dqkv = attend_back(qkv, first, perm_col, grad_attended, stat, cosine, sine)
    late_attn, late_grad, late_earlier, dqkv = lax.optimization_barrier(
        (after_attn, grad_out, earlier, dqkv)
    )
    part2, part3 = unproject(dqkv, perm_row, full_qkv, own_rows, 2)
    dp_count = lax.axis_size("dp")
    small = dp_count <= 8
    *parts, gain_partial = qkv_weights(
        normed_slot,
        dqkv,
        full_qkv,
        out_scattered,
        jnp.full((1,), lax.axis_index("dp") if small else 0, jnp.int32),
        dp_count if small else 1,
    )
    part0, part1 = unproject(dqkv, perm_row, full_qkv, own_rows, 0)
    grad_normed_attn = scatter_tensor([part0, part1, part2, part3])
    if small:
        grad_both = scatter_dp_parts(parts)
    else:
        grad_both = scatter_dp(parts[0])
    grad_qkv = grad_both[:, : 3 * head_cols]
    grad_out_t = grad_both[:, 3 * head_cols :]
    grad_gain_attn = gain_partial[:, 0] / gain_attn

    _, first_back = jax.vjp(lambda value: layer_norm(value, gain_attn), hidden)
    grad_hidden = (grad_after + first_back(grad_normed_attn)[0]).astype(bf16)

    cotangent = late_grad.astype(f32)
    block_out = late_attn + mlp_total
    prior = [late_earlier[index].astype(f32) for index in range(4)]
    mixed_total = mix_weights[4] * block_out
    for index in range(4):
        mixed_total = mixed_total + mix_weights[index] * prior[index]
    grad_earlier = (mix_weights[:4, None, None] * cotangent[None]).astype(bf16)
    mix_terms = [jnp.sum(cotangent * value) for value in prior + [block_out]]
    spare = -(2 * width + 5) % 1024
    packed = jnp.concatenate(
        [grad_gain_attn, grad_gain_mlp, jnp.stack(mix_terms), jnp.zeros((spare,), f32)]
    )
    packed = total_all(packed.reshape(-1, LANES)).reshape(-1)
    return (
        mixed_total.astype(bf16),
        grad_hidden,
        grad_earlier,
        packed[:width],
        packed[width : 2 * width],
        grad_qkv.reshape(shard_d, 3, head_cols),
        grad_out_t.T,
        grad_up,
        grad_down_t.T,
        packed[2 * width : 2 * width + 5],
    )


def solution(mesh):
    rows = P(("dp", "tensor"), None)
    layers = P(None, ("dp", "tensor"), None)
    return jax.shard_map(
        layer,
        mesh=mesh,
        in_specs=(
            rows,
            layers,
            P(),
            P(),
            P("dp", None, "tensor"),
            P("tensor", "dp"),
            P("dp", "tensor"),
            P("tensor", "dp"),
            P(),
            P("dp", None),
            P("dp"),
            rows,
        ),
        out_specs=(
            rows,
            rows,
            layers,
            P(),
            P(),
            P("dp", None, "tensor"),
            P("tensor", "dp"),
            P("dp", "tensor"),
            P("tensor", "dp"),
            P(),
        ),
        check_vma=False,
    )
```

```python
import jax
import jax.numpy as jnp
from jax import lax
from jax.experimental import pallas as pl
from jax.experimental.pallas import tpu as pltpu
from jax.sharding import PartitionSpec as P


HEAD_SIZE = 64
HALF = HEAD_SIZE // 2
LANES = 128
LOG2E = 1.4426950408889634
ROW_STEP = 256

eps = 1e-05
bf16 = jnp.bfloat16
f32 = jnp.float32


def layer_norm(value, gain):
    row_mean = jnp.mean(value, axis=-1, keepdims=True)
    centered = value - row_mean
    spread = jnp.mean(centered * centered, axis=-1, keepdims=True)
    return centered * lax.rsqrt(spread + eps) * gain


def slot_layout(lengths, slot_len):
    ends = jnp.cumsum(lengths, axis=-1)
    places = jnp.arange(slot_len, dtype=jnp.int32)
    passed = places[None, :, None] >= ends[:, None, :]
    first = jnp.max(jnp.where(passed, ends[:, None, :], 0), axis=-1)
    return (first, places[None, :] - first)


def angle_tables(position):
    inverse = 1.0 / 10000.0 ** (jnp.arange(HALF, dtype=f32) * (2.0 / HEAD_SIZE))
    phase_angle = position.astype(f32)[:, None] * inverse[None, :]
    cosine = jnp.cos(phase_angle)
    sine = jnp.sin(phase_angle)
    repeat = LANES // HEAD_SIZE
    return (
        jnp.concatenate([cosine, cosine] * repeat, axis=1),
        jnp.concatenate([-sine, sine] * repeat, axis=1),
    )


def swap_halves(value):
    lane = lax.broadcasted_iota(jnp.int32, value.shape, 1)
    low = (lane % HEAD_SIZE) < HALF
    return jnp.where(low, pltpu.roll(value, LANES - HALF, 1), pltpu.roll(value, HALF, 1))


def turn(value, cosine, sine):
    return value * cosine + swap_halves(value) * sine


def dot(a, b, dims=((1,), (0,))):
    return lax.dot_general(a, b, (dims, ((), ())), preferred_element_type=f32)


def order_kernel(n0, n1, n2, n3, perm_ref, slot_ref):
    slot_ref[...] = pick_rows(perm_ref[...], (n0, n1, n2, n3)).astype(bf16)


def pick_rows(wanted, pieces):
    each = pieces[0].shape[0]
    total = None
    for k in range(4):
        here = lax.broadcasted_iota(jnp.int32, (wanted.shape[0], each), 1) + k * each
        pick = jnp.where(here == wanted, 1.0, 0.0).astype(bf16)
        part = dot(pick, pieces[k][...])
        total = part if total is None else total + part
    return total


def to_slots(pieces, perm_col):
    each, width = pieces[0].shape
    rows = perm_col.shape[0]
    whole = pl.BlockSpec((each, width), lambda i: (0, 0))
    return pl.pallas_call(
        order_kernel,
        grid=(rows // ROW_STEP,),
        in_specs=[whole] * 4 + [pl.BlockSpec((ROW_STEP, 1), lambda i: (i, 0))],
        out_specs=pl.BlockSpec((ROW_STEP, width), lambda i: (i, 0)),
        out_shape=jax.ShapeDtypeStruct((rows, width), bf16),
        name="to_slots",
    )(*pieces, perm_col)


def project_kernel(normed_ref, w_ref, cos_ref, sin_ref, qkv_ref):
    normed = normed_ref[...]
    cosine = cos_ref[...]
    sine = sin_ref[...]
    third = w_ref.shape[2]
    both = jnp.concatenate([dot(normed, w_ref[0]), dot(normed, w_ref[1])], axis=1)
    for start in range(0, 2 * third, LANES):
        qkv_ref[:, start : start + LANES] = turn(
            both[:, start : start + LANES], cosine, sine
        ).astype(bf16)
    qkv_ref[:, 2 * third :] = dot(normed, w_ref[2]).astype(bf16)


def project(normed, w, cosine, sine):
    rows, width = normed.shape
    cols = 3 * w.shape[2]
    step = 2 * ROW_STEP
    return pl.pallas_call(
        project_kernel,
        grid=(rows // step,),
        in_specs=[
            pl.BlockSpec((step, width), lambda i: (i, 0)),
            pl.BlockSpec(w.shape, lambda i: (0, 0, 0)),
            pl.BlockSpec((step, LANES), lambda i: (i, 0)),
            pl.BlockSpec((step, LANES), lambda i: (i, 0)),
        ],
        out_specs=pl.BlockSpec((step, cols), lambda i: (i, 0)),
        out_shape=jax.ShapeDtypeStruct((rows, cols), bf16),
        name="project",
    )(normed, w, cosine, sine)


def norm_back(value, gain, grad):
    row_mean = jnp.mean(value, axis=-1, keepdims=True)
    centered = value - row_mean
    spread = jnp.mean(centered * centered, axis=-1, keepdims=True)
    rstd = lax.rsqrt(spread + eps)
    normed = centered * rstd
    scaled = grad * gain
    mean_scaled = jnp.mean(scaled, axis=-1, keepdims=True)
    mean_both = jnp.mean(scaled * normed, axis=-1, keepdims=True)
    return rstd * (scaled - mean_scaled - normed * mean_both), grad * normed


def added(a_ref, b_ref, c_ref):
    return a_ref[...].astype(f32) + b_ref[...].astype(f32) + c_ref[...].astype(f32)


def mid_back_kernel(
    mix_ref, value_ref, gain_ref, a_ref, b_ref, c_ref, grad_ref, w_ref, g_ref, low_ref, gain_out, *outs
):
    back, terms = norm_back(value_ref[...], gain_ref[...], added(a_ref, b_ref, c_ref))
    total = mix_ref[4] * grad_ref[...].astype(f32) + back
    low = total.astype(bf16)
    g_ref[...] = total
    low_ref[...] = low
    gain_out[0] = jnp.sum(terms, axis=0, keepdims=True)
    heads = dot(low, w_ref[...]).astype(bf16)
    cols = outs[0].shape[1]
    for k, ref in enumerate(outs):
        ref[...] = heads[:, k * cols : (k + 1) * cols]


def mid_back(mix, value, gain, grads, cotangent, w):
    rows, width = value.shape
    cols = w.shape[1] // 4
    steps = rows // ROW_STEP
    block = pl.BlockSpec((ROW_STEP, width), lambda i: (i, 0))
    return pl.pallas_call(
        mid_back_kernel,
        grid=(steps,),
        in_specs=[
            pl.BlockSpec(memory_space=pltpu.SMEM),
            block,
            pl.BlockSpec((1, width), lambda i: (0, 0)),
            block,
            block,
            block,
            block,
            pl.BlockSpec(w.shape, lambda i: (0, 0)),
        ],
        out_specs=[block, block, pl.BlockSpec((1, 1, width), lambda i: (i, 0, 0))]
        + [pl.BlockSpec((ROW_STEP, cols), lambda i: (i, 0))] * 4,
        out_shape=[
            jax.ShapeDtypeStruct((rows, width), f32),
            jax.ShapeDtypeStruct((rows, width), bf16),
            jax.ShapeDtypeStruct((steps, 1, width), f32),
        ]
        + [jax.ShapeDtypeStruct((rows, cols), bf16)] * 4,
        name="mid_back",
    )(mix, value, gain[None], *grads, cotangent, w)


def last_back_kernel(value_ref, gain_ref, a_ref, b_ref, c_ref, carry_ref, out_ref):
    back, _ = norm_back(value_ref[...].astype(f32), gain_ref[...], added(a_ref, b_ref, c_ref))
    out_ref[...] = (carry_ref[...] + back).astype(bf16)


def last_back(value, gain, grads, carry):
    rows, width = value.shape
    block = pl.BlockSpec((ROW_STEP, width), lambda i: (i, 0))
    return pl.pallas_call(
        last_back_kernel,
        grid=(rows // ROW_STEP,),
        in_specs=[block, pl.BlockSpec((1, width), lambda i: (0, 0))] + [block] * 4,
        out_specs=block,
        out_shape=jax.ShapeDtypeStruct((rows, width), bf16),
        name="last_back",
    )(value, gain[None], *grads, carry)


def mix_early_kernel(mix_ref, earlier_ref, grad_ref, out_ref, prior_ref, terms_ref):
    grad = grad_ref[...].astype(f32)
    prior = None
    for j in range(4):
        value = earlier_ref[j].astype(f32)
        out_ref[j] = (mix_ref[j] * grad).astype(bf16)
        terms_ref[0, j : j + 1, :] = jnp.sum(grad * value, axis=0, keepdims=True)
        part = mix_ref[j] * value
        prior = part if prior is None else prior + part
    prior_ref[...] = prior


def mix_early(mix, earlier, grad):
    rows, width = grad.shape
    steps = rows // ROW_STEP
    block = pl.BlockSpec((ROW_STEP, width), lambda i: (i, 0))
    layers = pl.BlockSpec((4, ROW_STEP, width), lambda i: (0, i, 0))
    return pl.pallas_call(
        mix_early_kernel,
        grid=(steps,),
        in_specs=[pl.BlockSpec(memory_space=pltpu.SMEM), layers, block],
        out_specs=[layers, block, pl.BlockSpec((1, 4, width), lambda i: (i, 0, 0))],
        out_shape=[
            jax.ShapeDtypeStruct(earlier.shape, bf16),
            jax.ShapeDtypeStruct((rows, width), f32),
            jax.ShapeDtypeStruct((steps, 4, width), f32),
        ],
        name="mix_early",
    )(mix, earlier, grad)


def mix_late_kernel(mix_ref, value_ref, a_ref, b_ref, c_ref, prior_ref, grad_ref, out_ref, term_ref):
    block_out = value_ref[...] + added(a_ref, b_ref, c_ref)
    out_ref[...] = (prior_ref[...] + mix_ref[4] * block_out).astype(bf16)
    term_ref[0] = jnp.sum(grad_ref[...].astype(f32) * block_out, axis=0, keepdims=True)


def mix_late(mix, value, terms, prior, grad):
    rows, width = grad.shape
    steps = rows // ROW_STEP
    block = pl.BlockSpec((ROW_STEP, width), lambda i: (i, 0))
    return pl.pallas_call(
        mix_late_kernel,
        grid=(steps,),
        in_specs=[pl.BlockSpec(memory_space=pltpu.SMEM)] + [block] * 6,
        out_specs=[block, pl.BlockSpec((1, 1, width), lambda i: (i, 0, 0))],
        out_shape=[
            jax.ShapeDtypeStruct((rows, width), bf16),
            jax.ShapeDtypeStruct((steps, 1, width), f32),
        ],
        name="mix_late",
    )(mix, value, *terms, prior, grad)


def mlp_kernel(a_ref, b_ref, ga_ref, gb_ref, up_ref, down_ref, *outs):
    c = 0.7978845608028654
    for n, (rows_ref, grad_ref) in enumerate(((a_ref, ga_ref), (b_ref, gb_ref))):
        dn_ref, hid_ref, du_ref = outs[3 * n : 3 * n + 3]
        u = dot(rows_ref[...], up_ref[...])
        square = u * u
        t = jnp.tanh(c * (u * (1.0 + 0.044715 * square)))
        half = 0.5 * (1.0 + t)
        hid_ref[...] = (u * half).astype(bf16)
        slope = half + 0.5 * u * (1.0 - t * t) * (c * (1.0 + 3 * 0.044715 * square))
        du = (dot(grad_ref[...], down_ref[...]) * slope).astype(bf16)
        du_ref[...] = du
        dn_ref[...] = dot(du, up_ref[...], ((1,), (1,))).astype(bf16)


def mlp(rows, grads, updown):
    each, width = rows[0].shape
    units = updown.shape[1] // 2
    block = pl.BlockSpec((ROW_STEP, width), lambda i: (i, 0))
    inner = pl.BlockSpec((ROW_STEP, units), lambda i: (i, 0))
    wide = jax.ShapeDtypeStruct((each, width), bf16)
    mid = jax.ShapeDtypeStruct((each, units), bf16)
    return pl.pallas_call(
        mlp_kernel,
        grid=(each // ROW_STEP,),
        in_specs=[block] * 4
        + [
            pl.BlockSpec((width, units), lambda i: (0, 0)),
            pl.BlockSpec((width, units), lambda i: (0, 1)),
        ],
        out_specs=[block, inner, inner] * 2,
        out_shape=[wide, mid, mid] * 2,
    )(*rows, *grads, updown, updown)


def mlp_out_kernel(h0, h1, h2, h3, down_ref, o0, o1, o2, o3):
    for hid_ref, out_ref in ((h3, o3), (h2, o2), (h1, o1), (h0, o0)):
        out_ref[...] = dot(hid_ref[...], down_ref[...], ((1,), (1,))).astype(bf16)


def mlp_out(hids, updown):
    each, units = hids[0].shape
    width = updown.shape[0]
    return pl.pallas_call(
        mlp_out_kernel,
        grid=(each // ROW_STEP,),
        in_specs=[pl.BlockSpec((ROW_STEP, units), lambda i: (i, 0))] * 4
        + [pl.BlockSpec((width, units), lambda i: (0, 1))],
        out_specs=[pl.BlockSpec((ROW_STEP, width), lambda i: (i, 0))] * 4,
        out_shape=[jax.ShapeDtypeStruct((each, width), bf16)] * 4,
        name="mlp_out",
    )(*hids, updown)


def mlp_weights_kernel(*refs):
    rows, grads, hids, dus = refs[:4], refs[4:8], refs[8:12], refs[12:16]
    out_ref, acc = refs[16:]
    units = hids[0].shape[1]
    step = pl.program_id(0)

    @pl.when(step == 0)
    def _():
        acc[...] = jnp.zeros(acc.shape, f32)

    up = down = None
    for k in range(4):
        a = dot(rows[k][...], dus[k][...], ((0,), (0,)))
        b = dot(grads[k][...], hids[k][...], ((0,), (0,)))
        up = a if up is None else up + a
        down = b if down is None else down + b
    acc[:, :units] += up
    acc[:, units:] += down

    @pl.when(step == pl.num_programs(0) - 1)
    def _():
        out_ref[...] = acc[...].astype(bf16)


def mlp_weights(rows, grads, hids, dus):
    each, width = rows[0].shape
    units = hids[0].shape[1]
    block = pl.BlockSpec((ROW_STEP, width), lambda i: (i, 0))
    inner = pl.BlockSpec((ROW_STEP, units), lambda i: (i, 0))
    return pl.pallas_call(
        mlp_weights_kernel,
        grid=(each // ROW_STEP,),
        in_specs=[block] * 8 + [inner] * 8,
        out_specs=pl.BlockSpec((width, 2 * units), lambda i: (0, 0)),
        out_shape=jax.ShapeDtypeStruct((width, 2 * units), bf16),
        scratch_shapes=[pltpu.VMEM((width, 2 * units), f32)],
        name="mlp_weights",
    )(*rows, *grads, *hids, *dus)


def spread_rows(perm_ref, value, start, count):
    total = value.shape[0]
    here = lax.broadcasted_iota(jnp.int32, (count, total), 0) + start
    pick = jnp.where(here == perm_ref[...], 1.0, 0.0).astype(bf16)
    return dot(pick, value)


def masked(scores, first_row, query_start):
    key = lax.broadcasted_iota(jnp.int32, scores.shape, 0)
    query = lax.broadcasted_iota(jnp.int32, scores.shape, 1) + query_start
    return jnp.where((key >= first_row) & (key <= query), scores, -1e30)


def attend_kernel(qkv_ref, first_ref, perm_ref, o0, o1, o2, o3, stat_ref, o_all):
    slot = pl.program_id(0)
    length, cols = qkv_ref.shape
    third = cols // 3
    factor = HEAD_SIZE ** (-0.5) * LOG2E
    for head in range(third // HEAD_SIZE):
        at = head * HEAD_SIZE
        key = qkv_ref[:, third + at : third + at + HEAD_SIZE]
        value = qkv_ref[:, 2 * third + at : 2 * third + at + HEAD_SIZE]
        value_t = value.T
        for start in range(0, length, ROW_STEP):
            seen = start + ROW_STEP
            query = qkv_ref[start:seen, at : at + HEAD_SIZE]
            scores = dot(key[:seen], query, ((1,), (1,)))
            scores = masked(scores, first_ref[0, :, start:seen], start)
            top = jnp.max(scores, axis=0, keepdims=True)
            weights = jnp.exp2((scores - top) * factor)
            mass = jnp.sum(weights, axis=0, keepdims=True)
            probs = (weights * (1.0 / mass)).astype(bf16)
            out = dot(value_t[:, :seen], probs).T
            stat_ref[0, head : head + 1, start:seen] = top * factor + jnp.log2(mass)
            o_all[pl.ds(slot * length + start, ROW_STEP), at : at + HEAD_SIZE] = out.astype(bf16)

    @pl.when(slot == pl.num_programs(0) - 1)
    def _():
        each = o0.shape[0]
        for k, ref in enumerate((o0, o1, o2, o3)):
            ref[...] = spread_rows(perm_ref, o_all[...], k * each, each).astype(bf16)


def attend(qkv, first, perm_row, each):
    slots, _, length = first.shape
    rows, cols = qkv.shape
    third = cols // 3
    piece = pl.BlockSpec((each, third), lambda i: (0, 0))
    return pl.pallas_call(
        attend_kernel,
        grid=(slots,),
        in_specs=[
            pl.BlockSpec((length, cols), lambda i: (i, 0)),
            pl.BlockSpec((1, 1, length), lambda i: (i, 0, 0)),
            pl.BlockSpec((1, rows), lambda i: (0, 0)),
        ],
        out_specs=[piece] * 4 + [pl.BlockSpec((1, 8, length), lambda i: (i, 0, 0))],
        out_shape=[jax.ShapeDtypeStruct((each, third), bf16)] * 4
        + [jax.ShapeDtypeStruct((slots, 8, length), f32)],
        scratch_shapes=[pltpu.VMEM((rows, third), bf16)],
        name="attend",
    )(qkv, first, perm_row)


def attend_back_kernel(
    qkv_ref, first_ref, perm_ref, d0, d1, d2, d3, stat_ref, cos_ref, sin_ref, out_ref, acc, given
):
    length, cols = qkv_ref.shape
    third = cols // 3
    scale = HEAD_SIZE ** (-0.5)
    factor = scale * LOG2E
    for start in range(0, length, ROW_STEP):
        wanted = perm_ref[start : start + ROW_STEP, :]
        given[start : start + ROW_STEP, :] = pick_rows(wanted, (d0, d1, d2, d3)).astype(bf16)
    acc[:, third:] = jnp.zeros((length, 2 * third), f32)
    for head in range(third // HEAD_SIZE):
        at = head * HEAD_SIZE
        key = qkv_ref[:, third + at : third + at + HEAD_SIZE]
        value = qkv_ref[:, 2 * third + at : 2 * third + at + HEAD_SIZE]
        key_t = key.T
        for start in range(0, length, ROW_STEP):
            seen = start + ROW_STEP
            query = qkv_ref[start:seen, at : at + HEAD_SIZE]
            grad = given[start:seen, at : at + HEAD_SIZE]
            scores = dot(key[:seen], query, ((1,), (1,)))
            scores = masked(scores, first_ref[0, :, start:seen], start)
            probs = jnp.exp2(scores * factor - stat_ref[0, head : head + 1, start:seen])
            grad_probs = dot(value[:seen], grad, ((1,), (1,)))
            delta = jnp.sum(probs * grad_probs, axis=0, keepdims=True)
            grad_scores = (probs * (grad_probs - delta)).astype(bf16)
            acc[start:seen, at : at + HEAD_SIZE] = dot(key_t[:, :seen], grad_scores).T
            acc[:seen, third + at : third + at + HEAD_SIZE] += dot(grad_scores, query)
            acc[:seen, 2 * third + at : 2 * third + at + HEAD_SIZE] += dot(
                probs.astype(bf16), grad
            )
    cosine = cos_ref[...]
    sine = -sin_ref[...]
    for start in range(0, 2 * third, LANES):
        out_ref[:, start : start + LANES] = turn(
            acc[:, start : start + LANES] * scale, cosine, sine
        ).astype(bf16)
    out_ref[:, 2 * third :] = acc[:, 2 * third :].astype(bf16)


def attend_back(qkv, first, perm_col, grads, stat, cosine, sine):
    slots, _, length = first.shape
    rows, cols = qkv.shape
    third = cols // 3
    piece = pl.BlockSpec(grads[0].shape, lambda i: (0, 0))
    return pl.pallas_call(
        attend_back_kernel,
        grid=(slots,),
        in_specs=[
            pl.BlockSpec((length, cols), lambda i: (i, 0)),
            pl.BlockSpec((1, 1, length), lambda i: (i, 0, 0)),
            pl.BlockSpec((length, 1), lambda i: (i, 0)),
        ]
        + [piece] * 4
        + [
            pl.BlockSpec((1, 8, length), lambda i: (i, 0, 0)),
            pl.BlockSpec((length, LANES), lambda i: (i, 0)),
            pl.BlockSpec((length, LANES), lambda i: (i, 0)),
        ],
        out_specs=pl.BlockSpec((length, cols), lambda i: (i, 0)),
        out_shape=jax.ShapeDtypeStruct((rows, cols), bf16),
        scratch_shapes=[pltpu.VMEM((length, cols), f32), pltpu.VMEM((length, third), bf16)],
        name="attend_back",
    )(qkv, first, perm_col, *grads, stat, cosine, sine)


def out_weights_kernel(grad_ref, *refs):
    grad = grad_ref[...]
    for k in range(4):
        refs[4 + k][...] = dot(grad, refs[k][...], ((0,), (0,))).astype(bf16)


def out_weights(grad, heads):
    width = grad.shape[1]
    cols = heads[0].shape[1]
    return pl.pallas_call(
        out_weights_kernel,
        out_shape=[jax.ShapeDtypeStruct((width, cols), bf16)] * 4,
        name="out_weights",
    )(grad, *heads)


def unproject(dqkv, perm_row, w, each, first):
    rows, cols = dqkv.shape
    width = w.shape[1]
    third = w.shape[2]

    def kernel(dqkv_ref, perm_ref, w_ref, a_ref, b_ref):
        for k, out_ref in ((first + 1, b_ref), (first, a_ref)):
            start = k * each + pl.program_id(0) * ROW_STEP
            picked = spread_rows(perm_ref, dqkv_ref[...], start, ROW_STEP).astype(bf16)
            total = dot(picked[:, :third], w_ref[0], ((1,), (1,)))
            total += dot(picked[:, third : 2 * third], w_ref[1], ((1,), (1,)))
            total += dot(picked[:, 2 * third :], w_ref[2], ((1,), (1,)))
            out_ref[...] = total.astype(bf16)

    return pl.pallas_call(
        kernel,
        grid=(each // ROW_STEP,),
        in_specs=[
            pl.BlockSpec((rows, cols), lambda i: (0, 0)),
            pl.BlockSpec((1, rows), lambda i: (0, 0)),
            pl.BlockSpec(w.shape, lambda i: (0, 0, 0)),
        ],
        out_specs=[pl.BlockSpec((ROW_STEP, width), lambda i: (i, 0))] * 2,
        out_shape=[jax.ShapeDtypeStruct((each, width), bf16)] * 2,
    )(dqkv, perm_row, w)


def hop(value, axis, bit):
    count = lax.axis_size(axis)
    return lax.ppermute(value, axis, [(i, i ^ bit) for i in range(count)])


def gather_tensor(value):
    near = hop(value, "tensor", 1)
    far = hop(value, "tensor", 2)
    cross = hop(far, "tensor", 1)
    return [value, near, far, cross]


def exchange_tensor(pieces):
    out = [pieces[0], hop(pieces[1], "tensor", 1)]
    return out + [hop(pieces[k], "tensor", k) for k in (2, 3)]


def fold_over(pieces):
    over = hop(pieces[1].astype(bf16), "tensor", 1)
    return (pieces[0].astype(f32) + over.astype(f32)).astype(bf16)


def fold_far(own, beside, outward):
    back = hop(outward, "tensor", 2)
    return [own, hop(beside.astype(bf16), "tensor", 1), back]


def scatter_tensor(pieces):
    return fold_far(pieces[0], pieces[1], fold_over(pieces[2:]))


def add_up(terms):
    total = terms[0].astype(f32)
    for term in terms[1:]:
        total = total + term.astype(f32)
    return total


def total_all(value):
    for axis in ("tensor", "dp"):
        bit = 1
        while bit < lax.axis_size(axis):
            value = value + hop(value, axis, bit)
            bit *= 2
    return value


def gather_dp(value):
    return lax.all_gather(value, "dp", axis=0, tiled=True)


def scatter_dp(value):
    return lax.psum_scatter(value.astype(bf16), "dp", scatter_dimension=0, tiled=True).astype(f32)


def gather_dp_steps(value):
    count = lax.axis_size("dp")
    kinds, share, cols = value.shape
    if count > 8:
        return lax.all_gather(value, "dp", axis=1, tiled=True)
    place = lax.axis_index("dp")
    bit = count // 2
    axis = 1
    while bit:
        other = hop(value, "dp", bit)
        upper = jnp.where((place & bit) > 0, 1, 0)
        shape = value.shape[:axis] + (2,) + value.shape[axis:]
        mine = lax.broadcasted_iota(jnp.int32, shape, axis) == upper
        value = jnp.where(mine, jnp.expand_dims(value, axis), jnp.expand_dims(other, axis))
        axis += 1
        bit //= 2
    return value.reshape(kinds, count * share, cols)


def scatter_dp_parts(parts):
    count = lax.axis_size("dp")
    parts = parts[:1] + [hop(parts[k], "dp", k) for k in range(1, count)]
    total = parts[0].astype(f32)
    for part in parts[1:]:
        total = total + part.astype(f32)
    return total


def qkv_weights_kernel(place_ref, normed_ref, dqkv_ref, w_ref, other_ref, *refs):
    parts, gain_ref, acc = refs[:-2], refs[-2], refs[-1]
    step = pl.program_id(0)
    cols = acc.shape[1]
    part = dot(normed_ref[...], dqkv_ref[...], ((0,), (0,)))

    @pl.when(step == 0)
    def _():
        acc[...] = part

    @pl.when(step > 0)
    def _():
        acc[...] += part

    @pl.when(step == pl.num_programs(0) - 1)
    def _():
        gain = None
        third = w_ref.shape[2]
        for c in range(3):
            term = acc[:, c * third : (c + 1) * third] * w_ref[c].astype(f32)
            gain = term if gain is None else gain + term
        gain_ref[...] = jnp.sum(gain, axis=1, keepdims=True)
        share = acc.shape[0] // len(parts)
        for k, ref in enumerate(parts):
            at = pl.multiple_of((place_ref[0] ^ k) * share, 8)
            ref[:, :cols] = acc[pl.ds(at, share), :].astype(bf16)
            ref[:, cols:] = other_ref[pl.ds(at, share), :].astype(bf16)


def qkv_weights(normed, dqkv, w, other, place, count):
    rows, width = normed.shape
    cols = dqkv.shape[1]
    extra = other.shape[1]
    step = 2 * ROW_STEP
    share = width // count
    return pl.pallas_call(
        qkv_weights_kernel,
        grid=(rows // step,),
        in_specs=[
            pl.BlockSpec(memory_space=pltpu.SMEM),
            pl.BlockSpec((step, width), lambda i: (i, 0)),
            pl.BlockSpec((step, cols), lambda i: (i, 0)),
            pl.BlockSpec(w.shape, lambda i: (0, 0, 0)),
            pl.BlockSpec(other.shape, lambda i: (0, 0)),
        ],
        out_specs=[pl.BlockSpec((share, cols + extra), lambda i: (0, 0))] * count
        + [pl.BlockSpec((width, 1), lambda i: (0, 0))],
        out_shape=[jax.ShapeDtypeStruct((share, cols + extra), bf16)] * count
        + [jax.ShapeDtypeStruct((width, 1), f32)],
        scratch_shapes=[pltpu.VMEM((width, cols), f32)],
        name="qkv_weights",
    )(place, normed, dqkv, w, other)


def layer(
    hidden_in,
    earlier,
    gain_attn,
    gain_mlp,
    w_qkv,
    w_out,
    w_up,
    w_down,
    mix_weights,
    lengths,
    slot_perm,
    grad_out,
):
    tensor_place = lax.axis_index("tensor")
    own_rows, width = hidden_in.shape
    slot_count = lengths.shape[0]
    group_rows = slot_perm.shape[0]
    slot_len = group_rows // slot_count
    shard_d = w_qkv.shape[0]
    head_cols = w_qkv.shape[2]

    hidden = hidden_in.astype(f32)
    normed_attn = layer_norm(hidden, gain_attn).astype(bf16)
    attn_pieces = gather_tensor(normed_attn)
    full_qkv = gather_dp_steps(jnp.transpose(w_qkv, (1, 0, 2)))
    out_pieces = gather_tensor(w_out.T)
    full_out = gather_dp(jnp.concatenate(out_pieces, axis=1))
    updown = gather_dp(jnp.concatenate([w_up, w_down.T], axis=1))

    first, position = slot_layout(lengths, slot_len)
    first = first.reshape(slot_count, 1, slot_len)
    cosine, sine = angle_tables(position.reshape(-1))
    perm = ((slot_perm // own_rows) ^ tensor_place) * own_rows + slot_perm % own_rows
    perm_col = perm[:, None]
    perm_row = perm[None, :]

    cotangent = grad_out.astype(f32)
    own_grad = mix_weights[4] * cotangent
    grad_pieces = gather_tensor(own_grad.astype(bf16))

    normed_slot = to_slots(attn_pieces, perm_col)
    qkv = project(normed_slot, full_qkv, cosine, sine)
    *attended, stat = attend(qkv, first, perm_row, own_rows)
    attended = exchange_tensor(attended)
    early_in, early_grad, attended[1] = lax.optimization_barrier((earlier, grad_out, attended[1]))
    grad_earlier, prior, prior_terms = mix_early(mix_weights, early_in, early_grad)
    heads_here = jnp.concatenate(attended, axis=1)
    after_attn = hidden + dot(heads_here, full_out, ((1,), (1,)))
    normed_mlp = layer_norm(after_attn, gain_mlp).astype(bf16)
    mlp_rows = gather_tensor(normed_mlp)

    dn0, hid0, du0, dn1, hid1, du1 = mlp(mlp_rows[:2], grad_pieces[:2], updown)
    dn2, hid2, du2, dn3, hid3, du3 = mlp(mlp_rows[2:], grad_pieces[2:], updown)
    mlp_terms = scatter_tensor([dn0, dn1, dn2, dn3])
    hids = [hid0, hid1, hid2, hid3]
    mlp_total = scatter_tensor(mlp_out(hids, updown))
    grad_updown = scatter_dp(mlp_weights(mlp_rows, grad_pieces, hids, [du0, du1, du2, du3]))
    units = w_up.shape[1]
    grad_up = grad_updown[:, :units]
    grad_down_t = grad_updown[:, units:]

    grad_after, grad_low, gain_rows, *grad_heads = mid_back(
        mix_weights, after_attn, gain_mlp, mlp_terms, grad_out, full_out
    )
    grad_gain_mlp = jnp.sum(gain_rows, axis=(0, 1))
    grad_attended = exchange_tensor(grad_heads)
    out_scattered = add_up(scatter_tensor(out_weights(grad_low, attended)))

    dqkv = attend_back(qkv, first, perm_col, grad_attended, stat, cosine, sine)
    part2, part3 = unproject(dqkv, perm_row, full_qkv, own_rows, 2)
    outward = fold_over([part2, part3])
    dp_count = lax.axis_size("dp")
    small = dp_count <= 8
    *parts, gain_partial = qkv_weights(
        normed_slot,
        dqkv,
        full_qkv,
        out_scattered,
        jnp.full((1,), lax.axis_index("dp") if small else 0, jnp.int32),
        dp_count if small else 1,
    )
    part0, part1 = unproject(dqkv, perm_row, full_qkv, own_rows, 0)
    attn_terms = fold_far(part0, part1, outward)
    late_prior, gain_partial, part1 = lax.optimization_barrier((prior, gain_partial, part1))
    if small:
        grad_both = scatter_dp_parts(parts)
    else:
        grad_both = scatter_dp(parts[0])
    grad_qkv = grad_both[:, : 3 * head_cols]
    grad_out_t = grad_both[:, 3 * head_cols :]
    grad_gain_attn = gain_partial[:, 0] / gain_attn

    grad_hidden = last_back(hidden_in, gain_attn, attn_terms, grad_after)

    mixed, last_term = mix_late(mix_weights, after_attn, mlp_total, late_prior, grad_out)
    mix_terms = jnp.concatenate([jnp.sum(prior_terms, axis=(0, 2)), jnp.sum(last_term)[None]])
    spare = -(2 * width + 5) % 1024
    packed = jnp.concatenate(
        [grad_gain_attn, grad_gain_mlp, mix_terms, jnp.zeros((spare,), f32)]
    )
    packed = total_all(packed.reshape(-1, LANES)).reshape(-1)
    return (
        mixed,
        grad_hidden,
        grad_earlier,
        packed[:width],
        packed[width : 2 * width],
        grad_qkv.reshape(shard_d, 3, head_cols),
        grad_out_t.T,
        grad_up,
        grad_down_t.T,
        packed[2 * width : 2 * width + 5],
    )


def solution(mesh):
    rows = P(("dp", "tensor"), None)
    layers = P(None, ("dp", "tensor"), None)
    return jax.shard_map(
        layer,
        mesh=mesh,
        in_specs=(
            rows,
            layers,
            P(),
            P(),
            P("dp", None, "tensor"),
            P("tensor", "dp"),
            P("dp", "tensor"),
            P("tensor", "dp"),
            P(),
            P("dp", None),
            P("dp"),
            rows,
        ),
        out_specs=(
            rows,
            rows,
            layers,
            P(),
            P(),
            P("dp", None, "tensor"),
            P("tensor", "dp"),
            P("dp", "tensor"),
            P("tensor", "dp"),
            P(),
        ),
        check_vma=False,
    )
```

```python
import jax
import jax.numpy as jnp
from jax import lax
from jax.experimental import pallas as pl
from jax.experimental.pallas import tpu as pltpu
from jax.sharding import PartitionSpec as P


TENSOR = "tensor"
DP = "dp"
HEAD_SIZE = 64
HALF = HEAD_SIZE // 2
LANES = 128
LOG2E = 1.4426950408889634
ROW_STEP = 256

eps = 1e-05
bf16 = jnp.bfloat16
f32 = jnp.float32


def layer_norm(value, gain):
    row_mean = jnp.mean(value, axis=-1, keepdims=True)
    centered = value - row_mean
    spread = jnp.mean(centered * centered, axis=-1, keepdims=True)
    return centered * lax.rsqrt(spread + eps) * gain


def slot_layout(lengths, slot_len):
    ends = jnp.cumsum(lengths, axis=-1)
    places = jnp.arange(slot_len, dtype=jnp.int32)
    passed = places[None, :, None] >= ends[:, None, :]
    first = jnp.max(jnp.where(passed, ends[:, None, :], 0), axis=-1)
    return (first, places[None, :] - first)


def angle_tables(position):
    inverse = 1.0 / 10000.0 ** (jnp.arange(HALF, dtype=f32) * (2.0 / HEAD_SIZE))
    phase_angle = position.astype(f32)[:, None] * inverse[None, :]
    cosine = jnp.cos(phase_angle)
    sine = jnp.sin(phase_angle)
    repeat = LANES // HEAD_SIZE
    return (
        jnp.concatenate([cosine, cosine] * repeat, axis=1),
        jnp.concatenate([-sine, sine] * repeat, axis=1),
    )


def swap_halves(value):
    lane = lax.broadcasted_iota(jnp.int32, value.shape, 1)
    low = (lane % HEAD_SIZE) < HALF
    return jnp.where(low, pltpu.roll(value, LANES - HALF, 1), pltpu.roll(value, HALF, 1))


def turn(value, cosine, sine):
    return value * cosine + swap_halves(value) * sine


def dot(a, b, dims=((1,), (0,))):
    return lax.dot_general(a, b, (dims, ((), ())), preferred_element_type=f32)


def order_kernel(n0, n1, n2, n3, perm_ref, slot_ref):
    slot_ref[...] = pick_rows(perm_ref[...], (n0, n1, n2, n3)).astype(bf16)


def pick_rows(wanted, pieces):
    each = pieces[0].shape[0]
    total = None
    for k in range(4):
        here = lax.broadcasted_iota(jnp.int32, (wanted.shape[0], each), 1) + k * each
        pick = jnp.where(here == wanted, 1.0, 0.0).astype(bf16)
        part = dot(pick, pieces[k][...])
        total = part if total is None else total + part
    return total


def to_slots(pieces, perm_col):
    each, width = pieces[0].shape
    rows = perm_col.shape[0]
    whole = pl.BlockSpec((each, width), lambda i: (0, 0))
    return pl.pallas_call(
        order_kernel,
        grid=(rows // ROW_STEP,),
        in_specs=[whole] * 4 + [pl.BlockSpec((ROW_STEP, 1), lambda i: (i, 0))],
        out_specs=pl.BlockSpec((ROW_STEP, width), lambda i: (i, 0)),
        out_shape=jax.ShapeDtypeStruct((rows, width), bf16),
        name="order",
    )(*pieces, perm_col)


def project_kernel(normed_ref, w_ref, cos_ref, sin_ref, qkv_ref):
    normed = normed_ref[...]
    cosine = cos_ref[...]
    sine = sin_ref[...]
    third = w_ref.shape[2]
    both = jnp.concatenate([dot(normed, w_ref[0]), dot(normed, w_ref[1])], axis=1)
    for start in range(0, 2 * third, LANES):
        qkv_ref[:, start : start + LANES] = turn(
            both[:, start : start + LANES], cosine, sine
        ).astype(bf16)
    qkv_ref[:, 2 * third :] = dot(normed, w_ref[2]).astype(bf16)


def project(normed, w, cosine, sine):
    rows, width = normed.shape
    cols = 3 * w.shape[2]
    step = 2 * ROW_STEP
    return pl.pallas_call(
        project_kernel,
        grid=(rows // step,),
        in_specs=[
            pl.BlockSpec((step, width), lambda i: (i, 0)),
            pl.BlockSpec((3,) + w.shape[1:], lambda i: (0, 0, 0)),
            pl.BlockSpec((step, LANES), lambda i: (i, 0)),
            pl.BlockSpec((step, LANES), lambda i: (i, 0)),
        ],
        out_specs=pl.BlockSpec((step, cols), lambda i: (i, 0)),
        out_shape=jax.ShapeDtypeStruct((rows, cols), bf16),
        name="proj",
    )(normed, w, cosine, sine)


def norm_back(value, gain, grad):
    row_mean = jnp.mean(value, axis=-1, keepdims=True)
    centered = value - row_mean
    spread = jnp.mean(centered * centered, axis=-1, keepdims=True)
    rstd = lax.rsqrt(spread + eps)
    normed = centered * rstd
    scaled = grad * gain
    mean_scaled = jnp.mean(scaled, axis=-1, keepdims=True)
    mean_both = jnp.mean(scaled * normed, axis=-1, keepdims=True)
    return rstd * (scaled - mean_scaled - normed * mean_both), grad * normed


def added(a_ref, b_ref, c_ref):
    return a_ref[...].astype(f32) + b_ref[...].astype(f32) + c_ref[...].astype(f32)


def mid_back_kernel(
    mix_ref, value_ref, gain_ref, a_ref, b_ref, c_ref, grad_ref, *refs
):
    weights, (g_ref, low_ref, gain_out, term_out), outs = refs[:4], refs[4:8], refs[8:]
    back, terms = norm_back(value_ref[...], gain_ref[...], added(a_ref, b_ref, c_ref))
    grad = grad_ref[...].astype(f32)
    total = mix_ref[4] * grad + back
    term_out[0] = jnp.sum(grad * value_ref[...], axis=0, keepdims=True)
    low = total.astype(bf16)
    g_ref[...] = total
    low_ref[...] = low
    gain_out[0] = jnp.sum(terms, axis=0, keepdims=True)
    for w_ref, ref in zip(weights, outs):
        ref[...] = dot(low, w_ref[...]).astype(bf16)


def mid_back(mix, value, gain, grads, cotangent, weights):
    rows, width = value.shape
    cols = weights[0].shape[1]
    steps = rows // ROW_STEP
    block = pl.BlockSpec((ROW_STEP, width), lambda i: (i, 0))
    return pl.pallas_call(
        mid_back_kernel,
        grid=(steps,),
        in_specs=[
            pl.BlockSpec(memory_space=pltpu.SMEM),
            block,
            pl.BlockSpec((1, width), lambda i: (0, 0)),
            block,
            block,
            block,
            block,
        ]
        + [pl.BlockSpec((width, cols), lambda i: (0, 0))] * 4,
        out_specs=[block, block] + [pl.BlockSpec((1, 1, width), lambda i: (i, 0, 0))] * 2
        + [pl.BlockSpec((ROW_STEP, cols), lambda i: (i, 0))] * 4,
        out_shape=[
            jax.ShapeDtypeStruct((rows, width), f32),
            jax.ShapeDtypeStruct((rows, width), bf16),
            jax.ShapeDtypeStruct((steps, 1, width), f32),
            jax.ShapeDtypeStruct((steps, 1, width), f32),
        ]
        + [jax.ShapeDtypeStruct((rows, cols), bf16)] * 4,
        name="mid_b",
    )(mix, value, gain[None], *grads, cotangent, *weights)


def last_back_kernel(value_ref, gain_ref, a_ref, b_ref, c_ref, carry_ref, out_ref):
    back, _ = norm_back(value_ref[...].astype(f32), gain_ref[...], added(a_ref, b_ref, c_ref))
    out_ref[...] = (carry_ref[...] + back).astype(bf16)


def last_back(value, gain, grads, carry):
    rows, width = value.shape
    block = pl.BlockSpec((ROW_STEP, width), lambda i: (i, 0))
    return pl.pallas_call(
        last_back_kernel,
        grid=(rows // ROW_STEP,),
        in_specs=[block, pl.BlockSpec((1, width), lambda i: (0, 0))] + [block] * 4,
        out_specs=block,
        out_shape=jax.ShapeDtypeStruct((rows, width), bf16),
        name="last_b",
    )(value, gain[None], *grads, carry)


def after_attn_kernel(value_ref, gain_ref, *refs):
    heads, weights, (total_ref, normed_ref) = refs[:4], refs[4:8], refs[8:]
    total = value_ref[...].astype(f32)
    for head_ref, w_ref in zip(heads, weights):
        total += dot(head_ref[...], w_ref[...], ((1,), (1,)))
    total_ref[...] = total
    normed_ref[...] = layer_norm(total, gain_ref[...]).astype(bf16)


def project_out(value, gain, heads, weights):
    rows, width = value.shape
    cols = heads[0].shape[1]
    block = pl.BlockSpec((ROW_STEP, width), lambda i: (i, 0))
    return pl.pallas_call(
        after_attn_kernel,
        grid=(rows // ROW_STEP,),
        in_specs=[block, pl.BlockSpec((1, width), lambda i: (0, 0))]
        + [pl.BlockSpec((ROW_STEP, cols), lambda i: (i, 0))] * 4
        + [pl.BlockSpec((width, cols), lambda i: (0, 0))] * 4,
        out_specs=[block, block],
        out_shape=[
            jax.ShapeDtypeStruct((rows, width), f32),
            jax.ShapeDtypeStruct((rows, width), bf16),
        ],
        name="proj_o",
    )(value, gain[None], *heads, *weights)


def mix_early_kernel(mix_ref, earlier_ref, grad_ref, out_ref, prior_ref, terms_ref):
    grad = grad_ref[...].astype(f32)
    prior = None
    for j in range(4):
        value = earlier_ref[j].astype(f32)
        out_ref[j] = (mix_ref[j] * grad).astype(bf16)
        terms_ref[0, j : j + 1, :] = jnp.sum(grad * value, axis=0, keepdims=True)
        part = mix_ref[j] * value
        prior = part if prior is None else prior + part
    prior_ref[...] = prior


def mix_early(mix, earlier, grad):
    rows, width = grad.shape
    steps = rows // ROW_STEP
    block = pl.BlockSpec((ROW_STEP, width), lambda i: (i, 0))
    layers = pl.BlockSpec((4, ROW_STEP, width), lambda i: (0, i, 0))
    return pl.pallas_call(
        mix_early_kernel,
        grid=(steps,),
        in_specs=[pl.BlockSpec(memory_space=pltpu.SMEM), layers, block],
        out_specs=[layers, block, pl.BlockSpec((1, 4, width), lambda i: (i, 0, 0))],
        out_shape=[
            jax.ShapeDtypeStruct(earlier.shape, bf16),
            jax.ShapeDtypeStruct((rows, width), f32),
            jax.ShapeDtypeStruct((steps, 4, width), f32),
        ],
        name="mix_e",
    )(mix, earlier, grad)


def mix_late_kernel(mix_ref, value_ref, a_ref, b_ref, c_ref, prior_ref, out_ref):
    block_out = value_ref[...] + added(a_ref, b_ref, c_ref)
    out_ref[...] = (prior_ref[...] + mix_ref[4] * block_out).astype(bf16)


def mix_late(mix, value, terms, prior):
    rows, width = value.shape
    block = pl.BlockSpec((ROW_STEP, width), lambda i: (i, 0))
    return pl.pallas_call(
        mix_late_kernel,
        grid=(rows // ROW_STEP,),
        in_specs=[pl.BlockSpec(memory_space=pltpu.SMEM)] + [block] * 5,
        out_specs=block,
        out_shape=jax.ShapeDtypeStruct((rows, width), bf16),
        name="mix_l",
    )(mix, value, *terms, prior)


def mlp_kernel(a_ref, b_ref, ga_ref, gb_ref, up_ref, down_ref, *outs):
    c = 0.7978845608028654
    for n, (rows_ref, grad_ref) in enumerate(((a_ref, ga_ref), (b_ref, gb_ref))):
        dn_ref, hid_ref, du_ref = outs[3 * n : 3 * n + 3]
        u = dot(rows_ref[...], up_ref[...])
        square = u * u
        t = jnp.tanh(c * (u * (1.0 + 0.044715 * square)))
        half = 0.5 * (1.0 + t)
        hid_ref[...] = (u * half).astype(bf16)
        slope = half + 0.5 * u * (1.0 - t * t) * (c * (1.0 + 3 * 0.044715 * square))
        du = (dot(grad_ref[...], down_ref[...]) * slope).astype(bf16)
        du_ref[...] = du
        dn_ref[...] = dot(du, up_ref[...], ((1,), (1,))).astype(bf16)


def mlp(rows, grads, updown):
    each, width = rows[0].shape
    units = updown.shape[1] // 2
    block = pl.BlockSpec((ROW_STEP, width), lambda i: (i, 0))
    inner = pl.BlockSpec((ROW_STEP, units), lambda i: (i, 0))
    wide = jax.ShapeDtypeStruct((each, width), bf16)
    mid = jax.ShapeDtypeStruct((each, units), bf16)
    return pl.pallas_call(
        mlp_kernel,
        grid=(each // ROW_STEP,),
        in_specs=[block] * 4
        + [
            pl.BlockSpec((width, units), lambda i: (0, 0)),
            pl.BlockSpec((width, units), lambda i: (0, 1)),
        ],
        out_specs=[block, inner, inner] * 2,
        out_shape=[wide, mid, mid] * 2,
    )(*rows, *grads, updown, updown)


def mlp_out_kernel(h0, h1, h2, h3, down_ref, o0, o1, o2, o3):
    for hid_ref, out_ref in ((h3, o3), (h2, o2), (h1, o1), (h0, o0)):
        out_ref[...] = dot(hid_ref[...], down_ref[...], ((1,), (1,))).astype(bf16)


def mlp_out(hids, updown):
    each, units = hids[0].shape
    width = updown.shape[0]
    return pl.pallas_call(
        mlp_out_kernel,
        grid=(each // ROW_STEP,),
        in_specs=[pl.BlockSpec((ROW_STEP, units), lambda i: (i, 0))] * 4
        + [pl.BlockSpec((width, units), lambda i: (0, 1))],
        out_specs=[pl.BlockSpec((ROW_STEP, width), lambda i: (i, 0))] * 4,
        out_shape=[jax.ShapeDtypeStruct((each, width), bf16)] * 4,
        name="mlp_out",
    )(*hids, updown)


def mlp_weights_kernel(*refs):
    rows, grads, hids, dus = refs[:4], refs[4:8], refs[8:12], refs[12:16]
    down_ref, out_ref, term_ref, acc = refs[16:]
    units = hids[0].shape[1]
    step = pl.program_id(0)

    @pl.when(step == 0)
    def _():
        acc[...] = jnp.zeros(acc.shape, f32)

    up = down = None
    for k in range(4):
        a = dot(rows[k][...], dus[k][...], ((0,), (0,)))
        b = dot(grads[k][...], hids[k][...], ((0,), (0,)))
        up = a if up is None else up + a
        down = b if down is None else down + b
    acc[:, :units] += up
    acc[:, units:] += down

    @pl.when(step == pl.num_programs(0) - 1)
    def _():
        out_ref[...] = acc[...].astype(bf16)
        term_ref[...] = jnp.sum(acc[:, units:] * down_ref[...].astype(f32), axis=0, keepdims=True)


def mlp_weights(rows, grads, hids, dus, updown):
    each, width = rows[0].shape
    units = hids[0].shape[1]
    block = pl.BlockSpec((ROW_STEP, width), lambda i: (i, 0))
    inner = pl.BlockSpec((ROW_STEP, units), lambda i: (i, 0))
    return pl.pallas_call(
        mlp_weights_kernel,
        grid=(each // ROW_STEP,),
        in_specs=[block] * 8 + [inner] * 8 + [pl.BlockSpec((width, units), lambda i: (0, 1))],
        out_specs=[
            pl.BlockSpec((width, 2 * units), lambda i: (0, 0)),
            pl.BlockSpec((1, units), lambda i: (0, 0)),
        ],
        out_shape=[
            jax.ShapeDtypeStruct((width, 2 * units), bf16),
            jax.ShapeDtypeStruct((1, units), f32),
        ],
        scratch_shapes=[pltpu.VMEM((width, 2 * units), f32)],
        name="wmlp",
    )(*rows, *grads, *hids, *dus, updown)


def spread_rows(perm_ref, value, start, count):
    total = value.shape[0]
    here = lax.broadcasted_iota(jnp.int32, (count, total), 0) + start
    pick = jnp.where(here == perm_ref[...], 1.0, 0.0).astype(bf16)
    return dot(pick, value)


def masked(scores, first_row, query_start):
    key = lax.broadcasted_iota(jnp.int32, scores.shape, 0)
    query = lax.broadcasted_iota(jnp.int32, scores.shape, 1) + query_start
    return jnp.where((key >= first_row) & (key <= query), scores, -1e30)


def attend_kernel(qkv_ref, first_ref, perm_ref, o0, o1, o2, o3, stat_ref, o_all):
    slot = pl.program_id(0)
    length, cols = qkv_ref.shape
    third = cols // 3
    factor = HEAD_SIZE ** (-0.5) * LOG2E
    for head in range(third // HEAD_SIZE):
        at = head * HEAD_SIZE
        key = qkv_ref[:, third + at : third + at + HEAD_SIZE]
        value = qkv_ref[:, 2 * third + at : 2 * third + at + HEAD_SIZE]
        value_t = value.T
        for start in range(0, length, ROW_STEP):
            seen = start + ROW_STEP
            query = qkv_ref[start:seen, at : at + HEAD_SIZE]
            scores = dot(key[:seen], query, ((1,), (1,)))
            scores = masked(scores, first_ref[0, :, start:seen], start)
            top = jnp.max(scores, axis=0, keepdims=True)
            weights = jnp.exp2((scores - top) * factor)
            mass = jnp.sum(weights, axis=0, keepdims=True)
            probs = (weights * (1.0 / mass)).astype(bf16)
            out = dot(value_t[:, :seen], probs).T
            stat_ref[0, head : head + 1, start:seen] = top * factor + jnp.log2(mass)
            o_all[pl.ds(slot * length + start, ROW_STEP), at : at + HEAD_SIZE] = out.astype(bf16)

    @pl.when(slot == pl.num_programs(0) - 1)
    def _():
        each = o0.shape[0]
        for k, ref in enumerate((o0, o1, o2, o3)):
            ref[...] = spread_rows(perm_ref, o_all[...], k * each, each).astype(bf16)


def attend(qkv, first, perm_row, each):
    slots, _, length = first.shape
    rows, cols = qkv.shape
    third = cols // 3
    piece = pl.BlockSpec((each, third), lambda i: (0, 0))
    return pl.pallas_call(
        attend_kernel,
        grid=(slots,),
        in_specs=[
            pl.BlockSpec((length, cols), lambda i: (i, 0)),
            pl.BlockSpec((1, 1, length), lambda i: (i, 0, 0)),
            pl.BlockSpec((1, rows), lambda i: (0, 0)),
        ],
        out_specs=[piece] * 4 + [pl.BlockSpec((1, 8, length), lambda i: (i, 0, 0))],
        out_shape=[jax.ShapeDtypeStruct((each, third), bf16)] * 4
        + [jax.ShapeDtypeStruct((slots, 8, length), f32)],
        scratch_shapes=[pltpu.VMEM((rows, third), bf16)],
        name="att",
    )(qkv, first, perm_row)


def attend_back_kernel(
    qkv_ref, first_ref, perm_ref, d0, d1, d2, d3, stat_ref, cos_ref, sin_ref, out_ref, acc, given
):
    length, cols = qkv_ref.shape
    third = cols // 3
    scale = HEAD_SIZE ** (-0.5)
    factor = scale * LOG2E
    for start in range(0, length, ROW_STEP):
        wanted = perm_ref[start : start + ROW_STEP, :]
        given[start : start + ROW_STEP, :] = pick_rows(wanted, (d0, d1, d2, d3)).astype(bf16)
    acc[:, third:] = jnp.zeros((length, 2 * third), f32)
    for head in range(third // HEAD_SIZE):
        at = head * HEAD_SIZE
        key = qkv_ref[:, third + at : third + at + HEAD_SIZE]
        value = qkv_ref[:, 2 * third + at : 2 * third + at + HEAD_SIZE]
        key_t = key.T
        for start in range(0, length, ROW_STEP):
            seen = start + ROW_STEP
            query = qkv_ref[start:seen, at : at + HEAD_SIZE]
            grad = given[start:seen, at : at + HEAD_SIZE]
            scores = dot(key[:seen], query, ((1,), (1,)))
            scores = masked(scores, first_ref[0, :, start:seen], start)
            probs = jnp.exp2(scores * factor - stat_ref[0, head : head + 1, start:seen])
            grad_probs = dot(value[:seen], grad, ((1,), (1,)))
            delta = jnp.sum(probs * grad_probs, axis=0, keepdims=True)
            grad_scores = (probs * (grad_probs - delta)).astype(bf16)
            acc[start:seen, at : at + HEAD_SIZE] = dot(key_t[:, :seen], grad_scores).T
            acc[:seen, third + at : third + at + HEAD_SIZE] += dot(grad_scores, query)
            acc[:seen, 2 * third + at : 2 * third + at + HEAD_SIZE] += dot(
                probs.astype(bf16), grad
            )
    cosine = cos_ref[...]
    sine = -sin_ref[...]
    for start in range(0, 2 * third, LANES):
        out_ref[:, start : start + LANES] = turn(
            acc[:, start : start + LANES] * scale, cosine, sine
        ).astype(bf16)
    out_ref[:, 2 * third :] = acc[:, 2 * third :].astype(bf16)


def attend_back(qkv, first, perm_col, grads, stat, cosine, sine):
    slots, _, length = first.shape
    rows, cols = qkv.shape
    third = cols // 3
    piece = pl.BlockSpec(grads[0].shape, lambda i: (0, 0))
    return pl.pallas_call(
        attend_back_kernel,
        grid=(slots,),
        in_specs=[
            pl.BlockSpec((length, cols), lambda i: (i, 0)),
            pl.BlockSpec((1, 1, length), lambda i: (i, 0, 0)),
            pl.BlockSpec((length, 1), lambda i: (i, 0)),
        ]
        + [piece] * 4
        + [
            pl.BlockSpec((1, 8, length), lambda i: (i, 0, 0)),
            pl.BlockSpec((length, LANES), lambda i: (i, 0)),
            pl.BlockSpec((length, LANES), lambda i: (i, 0)),
        ],
        out_specs=pl.BlockSpec((length, cols), lambda i: (i, 0)),
        out_shape=jax.ShapeDtypeStruct((rows, cols), bf16),
        scratch_shapes=[pltpu.VMEM((length, cols), f32), pltpu.VMEM((length, third), bf16)],
        name="att_b",
    )(qkv, first, perm_col, *grads, stat, cosine, sine)


def out_weights_kernel(grad_ref, *refs):
    grad = grad_ref[...]
    for k in range(4):
        refs[4 + k][...] = dot(grad, refs[k][...], ((0,), (0,))).astype(bf16)


def out_weights(grad, heads):
    width = grad.shape[1]
    cols = heads[0].shape[1]
    return pl.pallas_call(
        out_weights_kernel,
        out_shape=[jax.ShapeDtypeStruct((width, cols), bf16)] * 4,
        name="wout",
    )(grad, *heads)


def unproject(dqkv, perm_row, w, each, first):
    rows, cols = dqkv.shape
    width = w.shape[1]
    third = w.shape[2]

    def kernel(dqkv_ref, perm_ref, w_ref, a_ref, b_ref):
        for k, out_ref in ((first + 1, b_ref), (first, a_ref)):
            start = k * each + pl.program_id(0) * ROW_STEP
            picked = spread_rows(perm_ref, dqkv_ref[...], start, ROW_STEP).astype(bf16)
            total = dot(picked[:, :third], w_ref[0], ((1,), (1,)))
            total += dot(picked[:, third : 2 * third], w_ref[1], ((1,), (1,)))
            total += dot(picked[:, 2 * third :], w_ref[2], ((1,), (1,)))
            out_ref[...] = total.astype(bf16)

    return pl.pallas_call(
        kernel,
        grid=(each // ROW_STEP,),
        in_specs=[
            pl.BlockSpec((rows, cols), lambda i: (0, 0)),
            pl.BlockSpec((1, rows), lambda i: (0, 0)),
            pl.BlockSpec((3,) + w.shape[1:], lambda i: (0, 0, 0)),
        ],
        out_specs=[pl.BlockSpec((ROW_STEP, width), lambda i: (i, 0))] * 2,
        out_shape=[jax.ShapeDtypeStruct((each, width), bf16)] * 2,
    )(dqkv, perm_row, w)


def hop(value, axis, bit):
    count = lax.axis_size(axis)
    return lax.ppermute(value, axis, [(i, i ^ bit) for i in range(count)])


def gather_tensor(value):
    near = hop(value, TENSOR, 1)
    far = hop(value, TENSOR, 2)
    cross = hop(far, TENSOR, 1)
    return [value, near, far, cross]


def exchange_tensor(pieces):
    out = [pieces[0], hop(pieces[1], TENSOR, 1)]
    return out + [hop(pieces[k], TENSOR, k) for k in (2, 3)]


def fold_over(pieces):
    over = hop(pieces[1].astype(bf16), TENSOR, 1)
    return (pieces[0].astype(f32) + over.astype(f32)).astype(bf16)


def fold_far(own, beside, outward):
    back = hop(outward, TENSOR, 2)
    return [own, hop(beside.astype(bf16), TENSOR, 1), back]


def scatter_tensor(pieces):
    return fold_far(pieces[0], pieces[1], fold_over(pieces[2:]))


def add_up(terms):
    total = terms[0].astype(f32)
    for term in terms[1:]:
        total = total + term.astype(f32)
    return total


def total_all(value):
    for axis in (TENSOR, DP):
        bit = 1
        while bit < lax.axis_size(axis):
            value = value + hop(value, axis, bit)
            bit *= 2
    return value


def gather_dp(value):
    return lax.all_gather(value, DP, axis=0, tiled=True)


def scatter_dp(value):
    return lax.psum_scatter(value.astype(bf16), DP, scatter_dimension=0, tiled=True).astype(f32)


def gather_dp_steps(value, waiting):
    count = lax.axis_size(DP)
    kinds, share, cols = value.shape
    if count > 8:
        return lax.all_gather(value, DP, axis=1, tiled=True), waiting
    place = lax.axis_index(DP)
    bit = count // 2
    axis = 1
    while bit:
        other = hop(value, DP, bit)
        upper = jnp.where((place & bit) > 0, 1, 0)
        shape = value.shape[:axis] + (2,) + value.shape[axis:]
        mine = lax.broadcasted_iota(jnp.int32, shape, axis) == upper
        value = jnp.where(mine, jnp.expand_dims(value, axis), jnp.expand_dims(other, axis))
        if bit == 2:
            waiting, value = lax.optimization_barrier((waiting, value))
        axis += 1
        bit //= 2
    return value.reshape(kinds, count * share, cols), waiting


def scatter_dp_parts(parts):
    count = lax.axis_size(DP)
    parts = parts[:1] + [hop(parts[k], DP, k) for k in range(1, count)]
    total = parts[0].astype(f32)
    for part in parts[1:]:
        total = total + part.astype(f32)
    return total


def qkv_weights_kernel(place_ref, normed_ref, dqkv_ref, w_ref, other_ref, *refs):
    parts, gain_ref, acc = refs[:-2], refs[-2], refs[-1]
    step = pl.program_id(0)
    cols = acc.shape[1]
    part = dot(normed_ref[...], dqkv_ref[...], ((0,), (0,)))

    @pl.when(step == 0)
    def _():
        acc[...] = part

    @pl.when(step > 0)
    def _():
        acc[...] += part

    @pl.when(step == pl.num_programs(0) - 1)
    def _():
        gain = None
        third = w_ref.shape[2]
        for c in range(3):
            term = acc[:, c * third : (c + 1) * third] * w_ref[c].astype(f32)
            gain = term if gain is None else gain + term
        gain_ref[...] = jnp.sum(gain, axis=1, keepdims=True)
        share = acc.shape[0] // len(parts)
        for k, ref in enumerate(parts):
            at = pl.multiple_of((place_ref[0] ^ k) * share, 8)
            ref[:, :cols] = acc[pl.ds(at, share), :].astype(bf16)
            ref[:, cols:] = other_ref[pl.ds(at, share), :].astype(bf16)


def qkv_weights(normed, dqkv, w, other, place, count):
    rows, width = normed.shape
    cols = dqkv.shape[1]
    extra = other.shape[1]
    step = 2 * ROW_STEP
    share = width // count
    return pl.pallas_call(
        qkv_weights_kernel,
        grid=(rows // step,),
        in_specs=[
            pl.BlockSpec(memory_space=pltpu.SMEM),
            pl.BlockSpec((step, width), lambda i: (i, 0)),
            pl.BlockSpec((step, cols), lambda i: (i, 0)),
            pl.BlockSpec((3,) + w.shape[1:], lambda i: (0, 0, 0)),
            pl.BlockSpec(other.shape, lambda i: (0, 0)),
        ],
        out_specs=[pl.BlockSpec((share, cols + extra), lambda i: (0, 0))] * count
        + [pl.BlockSpec((width, 1), lambda i: (0, 0))],
        out_shape=[jax.ShapeDtypeStruct((share, cols + extra), bf16)] * count
        + [jax.ShapeDtypeStruct((width, 1), f32)],
        scratch_shapes=[pltpu.VMEM((width, cols), f32)],
        name="wqkv",
    )(place, normed, dqkv, w, other)


def layer(
    hidden_in,
    earlier,
    gain_attn,
    gain_mlp,
    w_qkv,
    w_out,
    w_up,
    w_down,
    mix_weights,
    lengths,
    slot_perm,
    grad_out,
):
    tensor_place = lax.axis_index(TENSOR)
    own_rows, width = hidden_in.shape
    slot_count = lengths.shape[0]
    group_rows = slot_perm.shape[0]
    slot_len = group_rows // slot_count
    shard_d = w_qkv.shape[0]
    head_cols = w_qkv.shape[2]

    hidden = hidden_in.astype(f32)
    normed_attn = layer_norm(hidden, gain_attn).astype(bf16)
    attn_pieces = gather_tensor(normed_attn)
    planes = jnp.concatenate([jnp.transpose(w_qkv, (1, 0, 2)), w_out.T[None]], axis=0)
    mlp_shard = jnp.concatenate([w_up, w_down.T], axis=1)
    full_qkv, mlp_shard = gather_dp_steps(planes, mlp_shard)
    updown = gather_dp(mlp_shard)
    out_pieces = gather_tensor(full_qkv[3])

    first, position = slot_layout(lengths, slot_len)
    first = first.reshape(slot_count, 1, slot_len)
    cosine, sine = angle_tables(position.reshape(-1))
    perm = ((slot_perm // own_rows) ^ tensor_place) * own_rows + slot_perm % own_rows
    perm_col = perm[:, None]
    perm_row = perm[None, :]

    cotangent = grad_out.astype(f32)
    own_grad = mix_weights[4] * cotangent
    grad_pieces = gather_tensor(own_grad.astype(bf16))

    normed_slot = to_slots(attn_pieces, perm_col)
    qkv = project(normed_slot, full_qkv, cosine, sine)
    *attended, stat = attend(qkv, first, perm_row, own_rows)
    attended = exchange_tensor(attended)
    early_in, early_grad, attended[1] = lax.optimization_barrier((earlier, grad_out, attended[1]))
    grad_earlier, prior, prior_terms = mix_early(mix_weights, early_in, early_grad)
    after_attn, normed_mlp = project_out(hidden_in, gain_mlp, attended, out_pieces)
    mlp_rows = gather_tensor(normed_mlp)

    dn0, hid0, du0, dn1, hid1, du1 = mlp(mlp_rows[:2], grad_pieces[:2], updown)
    dn2, hid2, du2, dn3, hid3, du3 = mlp(mlp_rows[2:], grad_pieces[2:], updown)
    mlp_terms = scatter_tensor([dn0, dn1, dn2, dn3])
    hids = [hid0, hid1, hid2, hid3]
    mlp_total = scatter_tensor(mlp_out(hids, updown))
    mlp_grads, down_terms = mlp_weights(
        mlp_rows, grad_pieces, hids, [du0, du1, du2, du3], updown
    )
    grad_updown = scatter_dp(mlp_grads)
    units = w_up.shape[1]
    grad_up = grad_updown[:, :units]
    grad_down_t = grad_updown[:, units:]

    grad_after, grad_low, gain_rows, own_terms, *grad_heads = mid_back(
        mix_weights, after_attn, gain_mlp, mlp_terms, grad_out, out_pieces
    )
    grad_gain_mlp = jnp.sum(gain_rows, axis=(0, 1))
    grad_attended = exchange_tensor(grad_heads)
    out_scattered = add_up(scatter_tensor(out_weights(grad_low, attended)))

    dqkv = attend_back(qkv, first, perm_col, grad_attended, stat, cosine, sine)
    part2, part3 = unproject(dqkv, perm_row, full_qkv, own_rows, 2)
    outward = fold_over([part2, part3])
    dp_count = lax.axis_size(DP)
    small = dp_count <= 8
    *parts, gain_partial = qkv_weights(
        normed_slot,
        dqkv,
        full_qkv,
        out_scattered,
        jnp.full((1,), lax.axis_index(DP) if small else 0, jnp.int32),
        dp_count if small else 1,
    )
    part0, part1 = unproject(dqkv, perm_row, full_qkv, own_rows, 0)
    attn_terms = fold_far(part0, part1, outward)
    late_prior, part1 = lax.optimization_barrier((prior, part1))
    if small:
        grad_both = scatter_dp_parts(parts)
    else:
        grad_both = scatter_dp(parts[0])
    grad_qkv = grad_both[:, : 3 * head_cols]
    grad_out_t = grad_both[:, 3 * head_cols :]
    grad_gain_attn = gain_partial[:, 0] / gain_attn

    grad_hidden = last_back(hidden_in, gain_attn, attn_terms, grad_after)

    mixed = mix_late(mix_weights, after_attn, mlp_total, late_prior)
    last_term = jnp.sum(own_terms) + jnp.sum(down_terms) / mix_weights[4]
    mix_terms = jnp.concatenate([jnp.sum(prior_terms, axis=(0, 2)), last_term[None]])
    spare = -(2 * width + 5) % 1024
    packed = jnp.concatenate(
        [grad_gain_attn, grad_gain_mlp, mix_terms, jnp.zeros((spare,), f32)]
    )
    packed = total_all(packed.reshape(-1, LANES)).reshape(-1)
    return (
        mixed,
        grad_hidden,
        grad_earlier,
        packed[:width],
        packed[width : 2 * width],
        grad_qkv.reshape(shard_d, 3, head_cols),
        grad_out_t.T,
        grad_up,
        grad_down_t.T,
        packed[2 * width : 2 * width + 5],
    )


def solution(mesh):
    rows = P((DP, TENSOR), None)
    layers = P(None, (DP, TENSOR), None)
    return jax.shard_map(
        layer,
        mesh=mesh,
        in_specs=(
            rows,
            layers,
            P(),
            P(),
            P(DP, None, TENSOR),
            P(TENSOR, DP),
            P(DP, TENSOR),
            P(TENSOR, DP),
            P(),
            P(DP, None),
            P(DP),
            rows,
        ),
        out_specs=(
            rows,
            rows,
            layers,
            P(),
            P(),
            P(DP, None, TENSOR),
            P(TENSOR, DP),
            P(DP, TENSOR),
            P(TENSOR, DP),
            P(),
        ),
        check_vma=False,
    )
```

```python
import jax
import jax.numpy as jnp
from jax import lax
from jax.experimental import pallas as pl
from jax.experimental.pallas import tpu as pltpu
from jax.sharding import PartitionSpec as P


TENSOR = "tensor"
DP = "dp"
HEAD_SIZE = 64
HALF = HEAD_SIZE // 2
LANES = 128
LOG2E = 1.4426950408889634
ROW_STEP = 256

eps = 1e-05
bf16 = jnp.bfloat16
f32 = jnp.float32


def layer_norm(value, gain):
    row_mean = jnp.mean(value, axis=-1, keepdims=True)
    centered = value - row_mean
    spread = jnp.mean(centered * centered, axis=-1, keepdims=True)
    return centered * lax.rsqrt(spread + eps) * gain


def slot_layout(lengths, slot_len):
    ends = jnp.cumsum(lengths, axis=-1)
    places = jnp.arange(slot_len, dtype=jnp.int32)
    passed = places[None, :, None] >= ends[:, None, :]
    first = jnp.max(jnp.where(passed, ends[:, None, :], 0), axis=-1)
    return (first, places[None, :] - first)


def angle_tables(position):
    inverse = 1.0 / 10000.0 ** (jnp.arange(HALF, dtype=f32) * (2.0 / HEAD_SIZE))
    phase_angle = position.astype(f32)[:, None] * inverse[None, :]
    cosine = jnp.cos(phase_angle)
    sine = jnp.sin(phase_angle)
    repeat = LANES // HEAD_SIZE
    return (
        jnp.concatenate([cosine, cosine] * repeat, axis=1),
        jnp.concatenate([-sine, sine] * repeat, axis=1),
    )


def swap_halves(value):
    lane = lax.broadcasted_iota(jnp.int32, value.shape, 1)
    low = (lane % HEAD_SIZE) < HALF
    return jnp.where(low, pltpu.roll(value, LANES - HALF, 1), pltpu.roll(value, HALF, 1))


def turn(value, cosine, sine):
    return value * cosine + swap_halves(value) * sine


def dot(a, b, dims=((1,), (0,))):
    return lax.dot_general(a, b, (dims, ((), ())), preferred_element_type=f32)


def order_kernel(n0, n1, n2, n3, perm_ref, slot_ref):
    slot_ref[...] = pick_rows(perm_ref[...], (n0, n1, n2, n3)).astype(bf16)


def pick_rows(wanted, pieces):
    each = pieces[0].shape[0]
    total = None
    for k in range(4):
        here = lax.broadcasted_iota(jnp.int32, (wanted.shape[0], each), 1) + k * each
        pick = jnp.where(here == wanted, 1.0, 0.0).astype(bf16)
        part = dot(pick, pieces[k][...])
        total = part if total is None else total + part
    return total


def to_slots(pieces, perm_col):
    each, width = pieces[0].shape
    rows = perm_col.shape[0]
    whole = pl.BlockSpec((each, width), lambda i: (0, 0))
    return pl.pallas_call(
        order_kernel,
        grid=(rows // ROW_STEP,),
        in_specs=[whole] * 4 + [pl.BlockSpec((ROW_STEP, 1), lambda i: (i, 0))],
        out_specs=pl.BlockSpec((ROW_STEP, width), lambda i: (i, 0)),
        out_shape=jax.ShapeDtypeStruct((rows, width), bf16),
        name="order",
    )(*pieces, perm_col)


def project_kernel(normed_ref, w_ref, cos_ref, sin_ref, qkv_ref):
    normed = normed_ref[...]
    cosine = cos_ref[...]
    sine = sin_ref[...]
    third = w_ref.shape[2]
    both = jnp.concatenate([dot(normed, w_ref[0]), dot(normed, w_ref[1])], axis=1)
    for start in range(0, 2 * third, LANES):
        qkv_ref[:, start : start + LANES] = turn(
            both[:, start : start + LANES], cosine, sine
        ).astype(bf16)
    qkv_ref[:, 2 * third :] = dot(normed, w_ref[2]).astype(bf16)


def project(normed, w, cosine, sine):
    rows, width = normed.shape
    cols = 3 * w.shape[2]
    step = 2 * ROW_STEP
    return pl.pallas_call(
        project_kernel,
        grid=(rows // step,),
        in_specs=[
            pl.BlockSpec((step, width), lambda i: (i, 0)),
            pl.BlockSpec((3,) + w.shape[1:], lambda i: (0, 0, 0)),
            pl.BlockSpec((step, LANES), lambda i: (i, 0)),
            pl.BlockSpec((step, LANES), lambda i: (i, 0)),
        ],
        out_specs=pl.BlockSpec((step, cols), lambda i: (i, 0)),
        out_shape=jax.ShapeDtypeStruct((rows, cols), bf16),
        name="proj",
    )(normed, w, cosine, sine)


def norm_back(value, gain, grad):
    row_mean = jnp.mean(value, axis=-1, keepdims=True)
    centered = value - row_mean
    spread = jnp.mean(centered * centered, axis=-1, keepdims=True)
    rstd = lax.rsqrt(spread + eps)
    normed = centered * rstd
    scaled = grad * gain
    mean_scaled = jnp.mean(scaled, axis=-1, keepdims=True)
    mean_both = jnp.mean(scaled * normed, axis=-1, keepdims=True)
    return rstd * (scaled - mean_scaled - normed * mean_both), grad * normed


def added(a_ref, b_ref, c_ref):
    return a_ref[...].astype(f32) + b_ref[...].astype(f32) + c_ref[...].astype(f32)


def mid_back_kernel(
    mix_ref, value_ref, gain_ref, a_ref, b_ref, c_ref, grad_ref, *refs
):
    weights, (g_ref, low_ref, gain_out, term_out), outs = refs[:4], refs[4:8], refs[8:]
    back, terms = norm_back(value_ref[...], gain_ref[...], added(a_ref, b_ref, c_ref))
    grad = grad_ref[...].astype(f32)
    total = mix_ref[4] * grad + back
    term_out[0] = jnp.sum(grad * value_ref[...], axis=0, keepdims=True)
    low = total.astype(bf16)
    g_ref[...] = total
    low_ref[...] = low
    gain_out[0] = jnp.sum(terms, axis=0, keepdims=True)
    for w_ref, ref in zip(weights, outs):
        ref[...] = dot(low, w_ref[...]).astype(bf16)


def mid_back(mix, value, gain, grads, cotangent, weights):
    rows, width = value.shape
    cols = weights[0].shape[1]
    steps = rows // ROW_STEP
    block = pl.BlockSpec((ROW_STEP, width), lambda i: (i, 0))
    return pl.pallas_call(
        mid_back_kernel,
        grid=(steps,),
        in_specs=[
            pl.BlockSpec(memory_space=pltpu.SMEM),
            block,
            pl.BlockSpec((1, width), lambda i: (0, 0)),
            block,
            block,
            block,
            block,
        ]
        + [pl.BlockSpec((width, cols), lambda i: (0, 0))] * 4,
        out_specs=[block, block] + [pl.BlockSpec((1, 1, width), lambda i: (i, 0, 0))] * 2
        + [pl.BlockSpec((ROW_STEP, cols), lambda i: (i, 0))] * 4,
        out_shape=[
            jax.ShapeDtypeStruct((rows, width), f32),
            jax.ShapeDtypeStruct((rows, width), bf16),
            jax.ShapeDtypeStruct((steps, 1, width), f32),
            jax.ShapeDtypeStruct((steps, 1, width), f32),
        ]
        + [jax.ShapeDtypeStruct((rows, cols), bf16)] * 4,
        name="mid_b",
    )(mix, value, gain[None], *grads, cotangent, *weights)


def last_back_kernel(value_ref, gain_ref, a_ref, b_ref, c_ref, carry_ref, out_ref):
    back, _ = norm_back(value_ref[...].astype(f32), gain_ref[...], added(a_ref, b_ref, c_ref))
    out_ref[...] = (carry_ref[...] + back).astype(bf16)


def last_back(value, gain, grads, carry):
    rows, width = value.shape
    block = pl.BlockSpec((ROW_STEP, width), lambda i: (i, 0))
    return pl.pallas_call(
        last_back_kernel,
        grid=(rows // ROW_STEP,),
        in_specs=[block, pl.BlockSpec((1, width), lambda i: (0, 0))] + [block] * 4,
        out_specs=block,
        out_shape=jax.ShapeDtypeStruct((rows, width), bf16),
        name="last_b",
    )(value, gain[None], *grads, carry)


def after_attn_kernel(value_ref, gain_ref, *refs):
    heads, weights, (total_ref, normed_ref) = refs[:4], refs[4:8], refs[8:]
    total = value_ref[...].astype(f32)
    for head_ref, w_ref in zip(heads, weights):
        total += dot(head_ref[...], w_ref[...], ((1,), (1,)))
    total_ref[...] = total
    normed_ref[...] = layer_norm(total, gain_ref[...]).astype(bf16)


def project_out(value, gain, heads, weights):
    rows, width = value.shape
    cols = heads[0].shape[1]
    block = pl.BlockSpec((ROW_STEP, width), lambda i: (i, 0))
    return pl.pallas_call(
        after_attn_kernel,
        grid=(rows // ROW_STEP,),
        in_specs=[block, pl.BlockSpec((1, width), lambda i: (0, 0))]
        + [pl.BlockSpec((ROW_STEP, cols), lambda i: (i, 0))] * 4
        + [pl.BlockSpec((width, cols), lambda i: (0, 0))] * 4,
        out_specs=[block, block],
        out_shape=[
            jax.ShapeDtypeStruct((rows, width), f32),
            jax.ShapeDtypeStruct((rows, width), bf16),
        ],
        name="proj_o",
    )(value, gain[None], *heads, *weights)


def mix_early_kernel(mix_ref, earlier_ref, grad_ref, out_ref, prior_ref, terms_ref):
    grad = grad_ref[...].astype(f32)
    prior = None
    for j in range(4):
        value = earlier_ref[j].astype(f32)
        out_ref[j] = (mix_ref[j] * grad).astype(bf16)
        terms_ref[0, j : j + 1, :] = jnp.sum(grad * value, axis=0, keepdims=True)
        part = mix_ref[j] * value
        prior = part if prior is None else prior + part
    prior_ref[...] = prior


def mix_early(mix, earlier, grad):
    rows, width = grad.shape
    steps = rows // ROW_STEP
    block = pl.BlockSpec((ROW_STEP, width), lambda i: (i, 0))
    layers = pl.BlockSpec((4, ROW_STEP, width), lambda i: (0, i, 0))
    return pl.pallas_call(
        mix_early_kernel,
        grid=(steps,),
        in_specs=[pl.BlockSpec(memory_space=pltpu.SMEM), layers, block],
        out_specs=[layers, block, pl.BlockSpec((1, 4, width), lambda i: (i, 0, 0))],
        out_shape=[
            jax.ShapeDtypeStruct(earlier.shape, bf16),
            jax.ShapeDtypeStruct((rows, width), f32),
            jax.ShapeDtypeStruct((steps, 4, width), f32),
        ],
        name="mix_e",
    )(mix, earlier, grad)


def mix_late_kernel(mix_ref, value_ref, a_ref, b_ref, c_ref, prior_ref, out_ref):
    block_out = value_ref[...] + added(a_ref, b_ref, c_ref)
    out_ref[...] = (prior_ref[...] + mix_ref[4] * block_out).astype(bf16)


def mix_late(mix, value, terms, prior):
    rows, width = value.shape
    block = pl.BlockSpec((ROW_STEP, width), lambda i: (i, 0))
    return pl.pallas_call(
        mix_late_kernel,
        grid=(rows // ROW_STEP,),
        in_specs=[pl.BlockSpec(memory_space=pltpu.SMEM)] + [block] * 5,
        out_specs=block,
        out_shape=jax.ShapeDtypeStruct((rows, width), bf16),
        name="mix_l",
    )(mix, value, *terms, prior)


def mlp_kernel(a_ref, b_ref, ga_ref, gb_ref, up_ref, down_ref, *outs):
    c = 0.7978845608028654
    for n, (rows_ref, grad_ref) in enumerate(((a_ref, ga_ref), (b_ref, gb_ref))):
        dn_ref, hid_ref, du_ref = outs[3 * n : 3 * n + 3]
        u = dot(rows_ref[...], up_ref[...])
        square = u * u
        t = jnp.tanh(c * (u * (1.0 + 0.044715 * square)))
        half = 0.5 * (1.0 + t)
        hid_ref[...] = (u * half).astype(bf16)
        slope = half + 0.5 * u * (1.0 - t * t) * (c * (1.0 + 3 * 0.044715 * square))
        du = (dot(grad_ref[...], down_ref[...]) * slope).astype(bf16)
        du_ref[...] = du
        dn_ref[...] = dot(du, up_ref[...], ((1,), (1,))).astype(bf16)


def mlp(rows, grads, updown):
    each, width = rows[0].shape
    units = updown.shape[1] // 2
    block = pl.BlockSpec((ROW_STEP, width), lambda i: (i, 0))
    inner = pl.BlockSpec((ROW_STEP, units), lambda i: (i, 0))
    wide = jax.ShapeDtypeStruct((each, width), bf16)
    mid = jax.ShapeDtypeStruct((each, units), bf16)
    return pl.pallas_call(
        mlp_kernel,
        grid=(each // ROW_STEP,),
        in_specs=[block] * 4
        + [
            pl.BlockSpec((width, units), lambda i: (0, 0)),
            pl.BlockSpec((width, units), lambda i: (0, 1)),
        ],
        out_specs=[block, inner, inner] * 2,
        out_shape=[wide, mid, mid] * 2,
    )(*rows, *grads, updown, updown)


def mlp_out_kernel(h0, h1, h2, h3, down_ref, o0, o1, o2, o3):
    for hid_ref, out_ref in ((h3, o3), (h2, o2), (h1, o1), (h0, o0)):
        out_ref[...] = dot(hid_ref[...], down_ref[...], ((1,), (1,))).astype(bf16)


def mlp_out(hids, updown):
    each, units = hids[0].shape
    width = updown.shape[0]
    return pl.pallas_call(
        mlp_out_kernel,
        grid=(each // ROW_STEP,),
        in_specs=[pl.BlockSpec((ROW_STEP, units), lambda i: (i, 0))] * 4
        + [pl.BlockSpec((width, units), lambda i: (0, 1))],
        out_specs=[pl.BlockSpec((ROW_STEP, width), lambda i: (i, 0))] * 4,
        out_shape=[jax.ShapeDtypeStruct((each, width), bf16)] * 4,
        name="mlp_out",
    )(*hids, updown)


def mlp_weights_kernel(*refs):
    rows, grads, hids, dus = refs[:4], refs[4:8], refs[8:12], refs[12:16]
    down_ref, out_ref, term_ref, acc = refs[16:]
    units = hids[0].shape[1]
    step = pl.program_id(0)

    @pl.when(step == 0)
    def _():
        acc[...] = jnp.zeros(acc.shape, f32)

    up = down = None
    for k in range(4):
        a = dot(rows[k][...], dus[k][...], ((0,), (0,)))
        b = dot(grads[k][...], hids[k][...], ((0,), (0,)))
        up = a if up is None else up + a
        down = b if down is None else down + b
    acc[:, :units] += up
    acc[:, units:] += down

    @pl.when(step == pl.num_programs(0) - 1)
    def _():
        out_ref[...] = acc[...].astype(bf16)
        term_ref[...] = jnp.sum(acc[:, units:] * down_ref[...].astype(f32), axis=0, keepdims=True)


def mlp_weights(rows, grads, hids, dus, updown):
    each, width = rows[0].shape
    units = hids[0].shape[1]
    block = pl.BlockSpec((ROW_STEP, width), lambda i: (i, 0))
    inner = pl.BlockSpec((ROW_STEP, units), lambda i: (i, 0))
    return pl.pallas_call(
        mlp_weights_kernel,
        grid=(each // ROW_STEP,),
        in_specs=[block] * 8 + [inner] * 8 + [pl.BlockSpec((width, units), lambda i: (0, 1))],
        out_specs=[
            pl.BlockSpec((width, 2 * units), lambda i: (0, 0)),
            pl.BlockSpec((1, units), lambda i: (0, 0)),
        ],
        out_shape=[
            jax.ShapeDtypeStruct((width, 2 * units), bf16),
            jax.ShapeDtypeStruct((1, units), f32),
        ],
        scratch_shapes=[pltpu.VMEM((width, 2 * units), f32)],
        name="wmlp",
    )(*rows, *grads, *hids, *dus, updown)


def spread_rows(perm_ref, value, start, count):
    total = value.shape[0]
    here = lax.broadcasted_iota(jnp.int32, (count, total), 0) + start
    pick = jnp.where(here == perm_ref[...], 1.0, 0.0).astype(bf16)
    return dot(pick, value)


def masked(scores, first_row, query_start):
    key = lax.broadcasted_iota(jnp.int32, scores.shape, 0)
    query = lax.broadcasted_iota(jnp.int32, scores.shape, 1) + query_start
    return jnp.where((key >= first_row) & (key <= query), scores, -1e30)


def attend_kernel(qkv_ref, first_ref, perm_ref, o0, o1, o2, o3, stat_ref, o_all):
    slot = pl.program_id(0)
    length, cols = qkv_ref.shape
    third = cols // 3
    factor = HEAD_SIZE ** (-0.5) * LOG2E
    for head in range(third // HEAD_SIZE):
        at = head * HEAD_SIZE
        key = qkv_ref[:, third + at : third + at + HEAD_SIZE]
        value = qkv_ref[:, 2 * third + at : 2 * third + at + HEAD_SIZE]
        value_t = value.T
        for start in range(0, length, ROW_STEP):
            seen = start + ROW_STEP
            query = qkv_ref[start:seen, at : at + HEAD_SIZE]
            scores = dot(key[:seen], query, ((1,), (1,)))
            scores = masked(scores, first_ref[0, :, start:seen], start)
            top = jnp.max(scores, axis=0, keepdims=True)
            weights = jnp.exp2((scores - top) * factor)
            mass = jnp.sum(weights, axis=0, keepdims=True)
            probs = (weights * (1.0 / mass)).astype(bf16)
            out = dot(value_t[:, :seen], probs).T
            stat_ref[0, head : head + 1, start:seen] = top * factor + jnp.log2(mass)
            o_all[pl.ds(slot * length + start, ROW_STEP), at : at + HEAD_SIZE] = out.astype(bf16)

    @pl.when(slot == pl.num_programs(0) - 1)
    def _():
        each = o0.shape[0]
        for k, ref in enumerate((o0, o1, o2, o3)):
            ref[...] = spread_rows(perm_ref, o_all[...], k * each, each).astype(bf16)


def attend(qkv, first, perm_row, each):
    slots, _, length = first.shape
    rows, cols = qkv.shape
    third = cols // 3
    piece = pl.BlockSpec((each, third), lambda i: (0, 0))
    return pl.pallas_call(
        attend_kernel,
        grid=(slots,),
        in_specs=[
            pl.BlockSpec((length, cols), lambda i: (i, 0)),
            pl.BlockSpec((1, 1, length), lambda i: (i, 0, 0)),
            pl.BlockSpec((1, rows), lambda i: (0, 0)),
        ],
        out_specs=[piece] * 4 + [pl.BlockSpec((1, 8, length), lambda i: (i, 0, 0))],
        out_shape=[jax.ShapeDtypeStruct((each, third), bf16)] * 4
        + [jax.ShapeDtypeStruct((slots, 8, length), f32)],
        scratch_shapes=[pltpu.VMEM((rows, third), bf16)],
        name="att",
    )(qkv, first, perm_row)


def attend_back_kernel(
    qkv_ref, first_ref, perm_ref, d0, d1, d2, d3, stat_ref, cos_ref, sin_ref, out_ref, acc, given
):
    length, cols = qkv_ref.shape
    third = cols // 3
    scale = HEAD_SIZE ** (-0.5)
    factor = scale * LOG2E
    for start in range(0, length, ROW_STEP):
        wanted = perm_ref[start : start + ROW_STEP, :]
        given[start : start + ROW_STEP, :] = pick_rows(wanted, (d0, d1, d2, d3)).astype(bf16)
    acc[:, third:] = jnp.zeros((length, 2 * third), f32)
    for head in range(third // HEAD_SIZE):
        at = head * HEAD_SIZE
        key = qkv_ref[:, third + at : third + at + HEAD_SIZE]
        value = qkv_ref[:, 2 * third + at : 2 * third + at + HEAD_SIZE]
        key_t = key.T
        for start in range(0, length, ROW_STEP):
            seen = start + ROW_STEP
            query = qkv_ref[start:seen, at : at + HEAD_SIZE]
            grad = given[start:seen, at : at + HEAD_SIZE]
            scores = dot(key[:seen], query, ((1,), (1,)))
            scores = masked(scores, first_ref[0, :, start:seen], start)
            probs = jnp.exp2(scores * factor - stat_ref[0, head : head + 1, start:seen])
            grad_probs = dot(value[:seen], grad, ((1,), (1,)))
            delta = jnp.sum(probs * grad_probs, axis=0, keepdims=True)
            grad_scores = (probs * (grad_probs - delta)).astype(bf16)
            acc[start:seen, at : at + HEAD_SIZE] = dot(key_t[:, :seen], grad_scores).T
            acc[:seen, third + at : third + at + HEAD_SIZE] += dot(grad_scores, query)
            acc[:seen, 2 * third + at : 2 * third + at + HEAD_SIZE] += dot(
                probs.astype(bf16), grad
            )
    cosine = cos_ref[...]
    sine = -sin_ref[...]
    for start in range(0, 2 * third, LANES):
        out_ref[:, start : start + LANES] = turn(
            acc[:, start : start + LANES] * scale, cosine, sine
        ).astype(bf16)
    out_ref[:, 2 * third :] = acc[:, 2 * third :].astype(bf16)


def attend_back(qkv, first, perm_col, grads, stat, cosine, sine):
    slots, _, length = first.shape
    rows, cols = qkv.shape
    third = cols // 3
    piece = pl.BlockSpec(grads[0].shape, lambda i: (0, 0))
    return pl.pallas_call(
        attend_back_kernel,
        grid=(slots,),
        in_specs=[
            pl.BlockSpec((length, cols), lambda i: (i, 0)),
            pl.BlockSpec((1, 1, length), lambda i: (i, 0, 0)),
            pl.BlockSpec((length, 1), lambda i: (i, 0)),
        ]
        + [piece] * 4
        + [
            pl.BlockSpec((1, 8, length), lambda i: (i, 0, 0)),
            pl.BlockSpec((length, LANES), lambda i: (i, 0)),
            pl.BlockSpec((length, LANES), lambda i: (i, 0)),
        ],
        out_specs=pl.BlockSpec((length, cols), lambda i: (i, 0)),
        out_shape=jax.ShapeDtypeStruct((rows, cols), bf16),
        scratch_shapes=[pltpu.VMEM((length, cols), f32), pltpu.VMEM((length, third), bf16)],
        name="att_b",
    )(qkv, first, perm_col, *grads, stat, cosine, sine)


def out_weights_kernel(grad_ref, *refs):
    grad = grad_ref[...]
    for k in range(4):
        refs[4 + k][...] = dot(grad, refs[k][...], ((0,), (0,))).astype(bf16)


def out_weights(grad, heads):
    width = grad.shape[1]
    cols = heads[0].shape[1]
    return pl.pallas_call(
        out_weights_kernel,
        out_shape=[jax.ShapeDtypeStruct((width, cols), bf16)] * 4,
        name="wout",
    )(grad, *heads)


def unproject(dqkv, perm_row, w, each, first):
    rows, cols = dqkv.shape
    width = w.shape[1]
    third = w.shape[2]

    def kernel(dqkv_ref, perm_ref, w_ref, a_ref, b_ref):
        for k, out_ref in ((first + 1, b_ref), (first, a_ref)):
            start = k * each + pl.program_id(0) * ROW_STEP
            picked = spread_rows(perm_ref, dqkv_ref[...], start, ROW_STEP).astype(bf16)
            total = dot(picked[:, :third], w_ref[0], ((1,), (1,)))
            total += dot(picked[:, third : 2 * third], w_ref[1], ((1,), (1,)))
            total += dot(picked[:, 2 * third :], w_ref[2], ((1,), (1,)))
            out_ref[...] = total.astype(bf16)

    return pl.pallas_call(
        kernel,
        grid=(each // ROW_STEP,),
        in_specs=[
            pl.BlockSpec((rows, cols), lambda i: (0, 0)),
            pl.BlockSpec((1, rows), lambda i: (0, 0)),
            pl.BlockSpec((3,) + w.shape[1:], lambda i: (0, 0, 0)),
        ],
        out_specs=[pl.BlockSpec((ROW_STEP, width), lambda i: (i, 0))] * 2,
        out_shape=[jax.ShapeDtypeStruct((each, width), bf16)] * 2,
    )(dqkv, perm_row, w)


def hop(value, axis, bit):
    count = lax.axis_size(axis)
    return lax.ppermute(value, axis, [(i, i ^ bit) for i in range(count)])


def gather_tensor(value):
    near = hop(value, TENSOR, 1)
    far = hop(value, TENSOR, 2)
    cross = hop(far, TENSOR, 1)
    return [value, near, far, cross]


def exchange_tensor(pieces):
    out = [pieces[0], hop(pieces[1], TENSOR, 1)]
    return out + [hop(pieces[k], TENSOR, k) for k in (2, 3)]


def fold_over(pieces):
    over = hop(pieces[1].astype(bf16), TENSOR, 1)
    return (pieces[0].astype(f32) + over.astype(f32)).astype(bf16)


def fold_far(own, beside, outward):
    back = hop(outward, TENSOR, 2)
    return [own, hop(beside.astype(bf16), TENSOR, 1), back]


def scatter_tensor(pieces):
    return fold_far(pieces[0], pieces[1], fold_over(pieces[2:]))


def fold_lanes(row, width):
    short = -row.shape[1] % width
    return jnp.sum(jnp.pad(row, ((0, 0), (0, short))).reshape(-1, width), axis=0, keepdims=True)


def total_all(value):
    for axis in (TENSOR, DP):
        bit = 1
        while bit < lax.axis_size(axis):
            value = value + hop(value, axis, bit)
            bit *= 2
    return value


def gather_dp(value):
    return lax.all_gather(value, DP, axis=0, tiled=True)


def scatter_dp(value):
    return lax.psum_scatter(value.astype(bf16), DP, scatter_dimension=0, tiled=True).astype(f32)


def gather_dp_steps(value, waiting):
    count = lax.axis_size(DP)
    kinds, share, cols = value.shape
    if count > 8:
        return lax.all_gather(value, DP, axis=1, tiled=True), waiting
    place = lax.axis_index(DP)
    bit = count // 2
    axis = 1
    while bit:
        other = hop(value, DP, bit)
        upper = jnp.where((place & bit) > 0, 1, 0)
        shape = value.shape[:axis] + (2,) + value.shape[axis:]
        mine = lax.broadcasted_iota(jnp.int32, shape, axis) == upper
        value = jnp.where(mine, jnp.expand_dims(value, axis), jnp.expand_dims(other, axis))
        if bit == 2:
            waiting, value = lax.optimization_barrier((waiting, value))
        axis += 1
        bit //= 2
    return value.reshape(kinds, count * share, cols), waiting


def scatter_dp_parts(parts):
    count = lax.axis_size(DP)
    parts = parts[:1] + [hop(parts[k], DP, k) for k in range(1, count)]
    total = parts[0].astype(f32)
    for part in parts[1:]:
        total = total + part.astype(f32)
    return total


def qkv_weights_kernel(
    place_ref, mix_ref, normed_ref, dqkv_ref, w_ref, a_ref, b_ref, c_ref, *refs
):
    gain_ref, rows_ref, own_ref, down_ref, prior_ref = refs[:5]
    parts, packed_ref, acc = refs[5:-2], refs[-2], refs[-1]
    step = pl.program_id(0)
    cols = acc.shape[1]
    part = dot(normed_ref[...], dqkv_ref[...], ((0,), (0,)))

    @pl.when(step == 0)
    def _():
        acc[...] = part

    @pl.when(step > 0)
    def _():
        acc[...] += part

    @pl.when(step == pl.num_programs(0) - 1)
    def _():
        product = None
        third = w_ref.shape[2]
        for c in range(3):
            term = acc[:, c * third : (c + 1) * third] * w_ref[c].astype(f32)
            product = term if product is None else product + term
        sums = lax.dot_general(
            jnp.ones((8, third), f32),
            product,
            (((1,), (1,)), ((), ())),
            precision=lax.Precision.HIGHEST,
            preferred_element_type=f32,
        )
        packed_ref[0:1, :] = sums[0:1, :] / gain_ref[...]
        packed_ref[1:2, :] = jnp.sum(rows_ref[...], axis=0)
        packed_ref[2:6, :] = jnp.sum(prior_ref[...], axis=0)
        packed_ref[6:7, :] = jnp.sum(own_ref[...], axis=0)
        packed_ref[7:8, :] = down_ref[...] / mix_ref[4]
        share = acc.shape[0] // len(parts)
        for k, ref in enumerate(parts):
            at = pl.multiple_of((place_ref[0] ^ k) * share, 8)
            ref[:, :cols] = acc[pl.ds(at, share), :].astype(bf16)
            here = pl.ds(at, share)
            other = a_ref[here, :].astype(f32) + b_ref[here, :].astype(f32)
            ref[:, cols:] = (other + c_ref[here, :].astype(f32)).astype(bf16)


def qkv_weights(normed, dqkv, w, others, smalls, mix, place, count):
    rows, width = normed.shape
    cols = dqkv.shape[1]
    extra = others[0].shape[1]
    step = 2 * ROW_STEP
    share = width // count

    def whole(array):
        return pl.BlockSpec(array.shape, lambda i: (0,) * array.ndim)

    return pl.pallas_call(
        qkv_weights_kernel,
        grid=(rows // step,),
        in_specs=[
            pl.BlockSpec(memory_space=pltpu.SMEM),
            pl.BlockSpec(memory_space=pltpu.SMEM),
            pl.BlockSpec((step, width), lambda i: (i, 0)),
            pl.BlockSpec((step, cols), lambda i: (i, 0)),
            pl.BlockSpec((3,) + w.shape[1:], lambda i: (0, 0, 0)),
        ]
        + [whole(array) for array in [*others, *smalls]],
        out_specs=[pl.BlockSpec((share, cols + extra), lambda i: (0, 0))] * count
        + [pl.BlockSpec((8, width), lambda i: (0, 0))],
        out_shape=[jax.ShapeDtypeStruct((share, cols + extra), bf16)] * count
        + [jax.ShapeDtypeStruct((8, width), f32)],
        scratch_shapes=[pltpu.VMEM((width, cols), f32)],
        name="wqkv",
    )(place, mix, normed, dqkv, w, *others, *smalls)


def layer(
    hidden_in,
    earlier,
    gain_attn,
    gain_mlp,
    w_qkv,
    w_out,
    w_up,
    w_down,
    mix_weights,
    lengths,
    slot_perm,
    grad_out,
):
    tensor_place = lax.axis_index(TENSOR)
    own_rows, width = hidden_in.shape
    slot_count = lengths.shape[0]
    group_rows = slot_perm.shape[0]
    slot_len = group_rows // slot_count
    shard_d = w_qkv.shape[0]
    head_cols = w_qkv.shape[2]

    hidden = hidden_in.astype(f32)
    normed_attn = layer_norm(hidden, gain_attn).astype(bf16)
    attn_pieces = gather_tensor(normed_attn)
    planes = jnp.concatenate([jnp.transpose(w_qkv, (1, 0, 2)), w_out.T[None]], axis=0)
    mlp_shard = jnp.concatenate([w_up, w_down.T], axis=1)
    full_qkv, mlp_shard = gather_dp_steps(planes, mlp_shard)
    updown = gather_dp(mlp_shard)
    out_pieces = gather_tensor(full_qkv[3])

    first, position = slot_layout(lengths, slot_len)
    first = first.reshape(slot_count, 1, slot_len)
    cosine, sine = angle_tables(position.reshape(-1))
    perm = ((slot_perm // own_rows) ^ tensor_place) * own_rows + slot_perm % own_rows
    perm_col = perm[:, None]
    perm_row = perm[None, :]

    cotangent = grad_out.astype(f32)
    own_grad = mix_weights[4] * cotangent
    grad_pieces = gather_tensor(own_grad.astype(bf16))

    normed_slot = to_slots(attn_pieces, perm_col)
    qkv = project(normed_slot, full_qkv, cosine, sine)
    *attended, stat = attend(qkv, first, perm_row, own_rows)
    attended = exchange_tensor(attended)
    early_in, early_grad, attended[1] = lax.optimization_barrier((earlier, grad_out, attended[1]))
    grad_earlier, prior, prior_terms = mix_early(mix_weights, early_in, early_grad)
    after_attn, normed_mlp = project_out(hidden_in, gain_mlp, attended, out_pieces)
    mlp_rows = gather_tensor(normed_mlp)

    dn0, hid0, du0, dn1, hid1, du1 = mlp(mlp_rows[:2], grad_pieces[:2], updown)
    dn2, hid2, du2, dn3, hid3, du3 = mlp(mlp_rows[2:], grad_pieces[2:], updown)
    mlp_terms = scatter_tensor([dn0, dn1, dn2, dn3])
    hids = [hid0, hid1, hid2, hid3]
    mlp_total = scatter_tensor(mlp_out(hids, updown))
    mlp_grads, down_terms = mlp_weights(
        mlp_rows, grad_pieces, hids, [du0, du1, du2, du3], updown
    )
    grad_updown = scatter_dp(mlp_grads)
    units = w_up.shape[1]
    grad_up = grad_updown[:, :units]
    grad_down_t = grad_updown[:, units:]

    grad_after, grad_low, gain_rows, own_terms, *grad_heads = mid_back(
        mix_weights, after_attn, gain_mlp, mlp_terms, grad_out, out_pieces
    )
    grad_attended = exchange_tensor(grad_heads)
    out_terms = scatter_tensor(out_weights(grad_low, attended))

    dqkv = attend_back(qkv, first, perm_col, grad_attended, stat, cosine, sine)
    part2, part3 = unproject(dqkv, perm_row, full_qkv, own_rows, 2)
    outward = fold_over([part2, part3])
    dp_count = lax.axis_size(DP)
    small = dp_count <= 8
    *parts, packed = qkv_weights(
        normed_slot,
        dqkv,
        full_qkv,
        out_terms,
        (gain_attn[None], gain_rows, own_terms, fold_lanes(down_terms, width), prior_terms),
        mix_weights,
        jnp.full((1,), lax.axis_index(DP) if small else 0, jnp.int32),
        dp_count if small else 1,
    )
    part0, part1 = unproject(dqkv, perm_row, full_qkv, own_rows, 0)
    attn_terms = fold_far(part0, part1, outward)
    late_prior, part1 = lax.optimization_barrier((prior, part1))
    if small:
        grad_both = scatter_dp_parts(parts)
    else:
        grad_both = scatter_dp(parts[0])
    grad_qkv = grad_both[:, : 3 * head_cols]
    grad_out_t = grad_both[:, 3 * head_cols :]

    grad_hidden = last_back(hidden_in, gain_attn, attn_terms, grad_after)

    mixed = mix_late(mix_weights, after_attn, mlp_total, late_prior)
    packed = total_all(packed)
    lane_sums = jnp.sum(packed[2:8], axis=1)
    grad_mix = jnp.concatenate([lane_sums[:4], lane_sums[4:5] + lane_sums[5:6]])
    return (
        mixed,
        grad_hidden,
        grad_earlier,
        packed[0],
        packed[1],
        grad_qkv.reshape(shard_d, 3, head_cols),
        grad_out_t.T,
        grad_up,
        grad_down_t.T,
        grad_mix,
    )


def solution(mesh):
    rows = P((DP, TENSOR), None)
    layers = P(None, (DP, TENSOR), None)
    return jax.shard_map(
        layer,
        mesh=mesh,
        in_specs=(
            rows,
            layers,
            P(),
            P(),
            P(DP, None, TENSOR),
            P(TENSOR, DP),
            P(DP, TENSOR),
            P(TENSOR, DP),
            P(),
            P(DP, None),
            P(DP),
            rows,
        ),
        out_specs=(
            rows,
            rows,
            layers,
            P(),
            P(),
            P(DP, None, TENSOR),
            P(TENSOR, DP),
            P(DP, TENSOR),
            P(TENSOR, DP),
            P(),
        ),
        check_vma=False,
    )
```
